32 devices in a mesh: layer: 4 (over y, x), dp: 8 (over z, core).
Axes of the slice: x: 2, y: 2, z: 4, core: 2. Of those that a mesh axis runs over, the one named last changes fastest.
Arguments:
- states: bfloat16 [8, 16, 32, 32, 256], P('layer', 'dp'), may hold values from -6 to 6
- slopes: bfloat16 [8, 16, 32, 32, 256], P('layer', 'dp'), may hold values from 0.099609375 to 1
- kernels: bfloat16 [8, 9, 256, 256], P('layer'), may hold values from -0.125 to 0.125
- guess: float32 [8, 16, 32, 32, 256], P('layer', 'dp'), may hold values from -6 to 6
Outputs:
- lower_adjoint: float32 [4, 16, 32, 32, 256], P('layer', 'dp')
- kernel_grad: float32 [8, 9, 256, 256], P('layer', None, 'dp')
The draws below stay inside these ranges and needn't reach their ends.
All inputs are finite; a program needn't handle non-finite values.
Results may differ from the reference program's by a relative error of at most 0.005.
Values sent between devices are 32-bit elements; how exact they have to be, the bound alone decides.
No kernel may reach another device: no remote copies, remote signals or barrier semaphores. Data moves between devices by JAX's collectives and lax.ppermute only.
A program may use at most 64 MiB of HBM per device.

```python
import jax
import jax.numpy as jnp

C = 256
HEIGHT = 32
WIDTH = 32
L_DEV = 2
IMAGES = 16
LAYERS = 8
N_LAYER = 4


def with_spikes(array, own_key, source, target, blocks, factor):
    owner, partner = [(jnp.arange(array.shape[dim]) // (array.shape[dim] // blocks)).reshape([-1 if axis == dim else 1 for axis in range(array.ndim)]) for dim in (source, target)]
    chosen = jax.random.permutation(own_key, blocks)[partner]
    strong = (owner == chosen) | (owner == (partner + blocks // 2) % blocks)
    return jnp.where(strong, factor * array, array)


def level_of(own_key, shape, split, smallest, largest):
    def one(dim, blocks):
        steps = jax.random.uniform(jax.random.fold_in(jax.random.fold_in(own_key, 6), dim), (blocks,), jnp.float32, smallest / len(split), largest / len(split))
        return jnp.repeat(jnp.exp(steps), shape[dim] // blocks).reshape((-1,) + (1,) * (len(shape) - dim - 1))

    factor_of = one(*split[0])
    for cut in split[1:]:
        factor_of = factor_of * one(*cut)
    return factor_of


def scatter_about(rng, shape, deviation, most, cuts=(), dtype=jnp.bfloat16):
    array = deviation * jax.random.normal(rng, shape, jnp.float32)
    if cuts:
        array = array * level_of(rng, shape, cuts, -0.22, 0.18)
    return jnp.clip(array, -most, most).astype(dtype)


def heavy_noise(stream_key, shape, spread, reach, cuts, heavy, dtype=jnp.bfloat16):
    entries = spread * jax.random.normal(stream_key, shape, jnp.float32)
    if cuts:
        entries = entries * level_of(stream_key, shape, cuts, -0.22, 0.18)
    return jnp.clip(with_spikes(entries, jax.random.fold_in(stream_key, 3), *heavy), -reach, reach).astype(dtype)


def setup_inputs(seed: int = 0) -> dict:
    streams_of = jax.random.split(jax.random.key(seed), 5)
    states = heavy_noise(streams_of[0], (LAYERS, IMAGES, HEIGHT, WIDTH, C), 1.0, 6.0, ((0, 4), (1, 8)), (1, 4, 8, 2.0))
    slopes = jnp.clip(0.099609375 + 0.9003906 * jax.random.uniform(streams_of[1], (LAYERS, IMAGES, HEIGHT, WIDTH, C), jnp.float32) ** level_of(streams_of[1], (LAYERS, IMAGES, HEIGHT, WIDTH, C), ((0, 4), (1, 8)), -0.2, 0.2), 0.099609375, 1.0).astype(jnp.bfloat16)
    kernels = scatter_about(streams_of[2], (LAYERS, 9, C, C), (9 * C) ** -0.5, 0.125, ((0, 4),))
    guess = scatter_about(streams_of[3], (LAYERS, IMAGES, HEIGHT, WIDTH, C), 1.0, 6.0, ((0, 4), (1, 8)), jnp.float32)
    return {"states": states, "slopes": slopes, "kernels": kernels, "guess": guess}


step_size = 0.5


def padded_float(images):
    return jnp.pad(images.astype(jnp.float32), ((0, 0), (1, 1), (1, 1), (0, 0)))


def transpose_conv(cotangent, kernel):
    image_count = cotangent.shape[0]
    image_height = cotangent.shape[1]
    image_width = cotangent.shape[2]
    channels = cotangent.shape[3]
    padded = padded_float(cotangent)
    kernel_float = kernel.astype(jnp.float32)
    total = jnp.zeros((image_count * image_height * image_width, channels), jnp.float32)
    for row_shift in range(3):
        for col_shift in range(3):
            piece = padded[:, 2 - row_shift:2 - row_shift + image_height, 2 - col_shift:2 - col_shift + image_width, :]
            piece = piece.reshape(image_count * image_height * image_width, channels)
            total = total + jnp.dot(piece, kernel_float[3 * row_shift + col_shift].T, preferred_element_type=jnp.float32)
    return total.reshape(cotangent.shape)


def correlate(inputs, cotangent):
    image_count = inputs.shape[0]
    image_height = inputs.shape[1]
    image_width = inputs.shape[2]
    channels = inputs.shape[3]
    padded = padded_float(inputs)
    rows = image_count * image_height * image_width
    cot_rows = cotangent.astype(jnp.float32).reshape(rows, channels)
    taps = []
    for row_shift in range(3):
        for col_shift in range(3):
            piece = padded[:, row_shift:row_shift + image_height, col_shift:col_shift + image_width, :].reshape(rows, channels)
            taps.append(jnp.dot(piece.T, cot_rows, preferred_element_type=jnp.float32))
    return jnp.stack(taps)


def apply_layer(adjoint, slope, kernel, factor):
    cotangent = (slope.astype(jnp.float32) * adjoint).astype(jnp.bfloat16)
    return adjoint + factor * transpose_conv(cotangent, kernel), cotangent


def reference(states, slopes, kernels, guess):
    sections = N_LAYER
    layer_count = L_DEV
    images = states.shape[1]
    carried = [jnp.zeros(guess.shape[1:], jnp.float32) for section in range(sections)]
    following = jnp.zeros(guess.shape[1:], jnp.float32)
    for section in range(sections - 1, 0, -1):
        bottom = section * layer_count
        section_end, unused = apply_layer(guess[bottom], slopes[bottom], kernels[bottom], step_size)
        coarse, unused = apply_layer(following, slopes[bottom], kernels[bottom], step_size * layer_count)
        following = (coarse + section_end) - guess[bottom - 1]
        carried[section - 1] = following
    lowers = []
    gradients = [None] * (sections * layer_count)
    for section in range(sections):
        adjoint = guess[section * layer_count + layer_count - 1] + carried[section]
        for inner_layer in range(layer_count - 1, -1, -1):
            layer_index = section * layer_count + inner_layer
            adjoint, cotangent = apply_layer(adjoint, slopes[layer_index], kernels[layer_index], step_size)
            gradients[layer_index] = correlate(states[layer_index], cotangent) * (step_size / images)
        lowers.append(adjoint)
    return jnp.stack(lowers), jnp.stack(gradients)
```

```python
import functools

import jax
import jax.numpy as jnp
from jax import lax
from jax.experimental import pallas as pl
from jax.experimental.pallas import tpu as pltpu
from jax.sharding import PartitionSpec as P


PIECES = 4

step_size = 0.5

f32 = jnp.float32
bf16 = jnp.bfloat16


def tile_of(size):
    for tile in (256, 128, 64, 32):
        if size % tile == 0:
            return tile
    return size


def fill(zs, first, z, width):
    count = z.shape[0]
    column = lax.broadcasted_iota(jnp.int32, z.shape, 0) % width
    after = jnp.where(column == width - 1, 0.0, pltpu.roll(z, count - 1, 0))
    before = jnp.where(column == 0, 0.0, pltpu.roll(z, 1, 0))
    rows = pl.ds(first, count)
    zs[0, rows, :] = after.astype(bf16)
    zs[1, rows, :] = z.astype(bf16)
    zs[2, rows, :] = before.astype(bf16)


def blank(zs, first, count):
    zs[:, pl.ds(first, count), :] = jnp.zeros((3, count, zs.shape[2]), bf16)


def taps_at(zs, kernel_ref, start, size, width):
    total = None
    for a in range(3):
        for b in range(3):
            rows = zs[b, pl.ds(start + (2 - a) * width, size), :]
            term = lax.dot_general(
                rows, kernel_ref[3 * a + b], (((1,), (1,)), ((), ())), preferred_element_type=f32
            )
            total = term if total is None else total + term
    return total


def conv_into(out, zs, kernel_ref, width, finish):
    count = out.shape[0]
    tile = tile_of(count)
    for start in range(0, count, tile):
        out[pl.ds(start, tile), :] = finish(start, tile, taps_at(zs, kernel_ref, start, tile, width))


def window(shape, lead, first):
    spec = (None,) * len(lead) + (pl.Element(shape[0]), pl.Element(shape[1]))
    return pl.BlockSpec(spec, lambda *_: (*lead, first, 0))


def cost(rows, channels, taps, moved):
    return pl.CostEstimate(
        flops=2 * rows * channels * channels * taps, bytes_accessed=moved, transcendentals=0
    )


def whole(shape):
    return pl.BlockSpec(shape, lambda *_: (0,) * len(shape))


def end_kernel(width, guess, slope, kernel, out, zs):
    count = guess.shape[0]
    blank(zs, 0, width)
    blank(zs, count + width, width)
    fill(zs, width, slope[...].astype(f32) * guess[...], width)
    conv_into(
        out, zs, kernel, width,
        lambda s, n, moved: guess[pl.ds(s, n), :] + step_size * moved,
    )


def section_end_of(guess, slopes, kernels, image, width):
    pixels, channels = guess.shape[2:]
    return pl.pallas_call(
        functools.partial(end_kernel, width),
        out_shape=jax.ShapeDtypeStruct((pixels, channels), f32),
        grid=(1,),
        in_specs=[
            window((pixels, channels), (0, image), 0),
            window((pixels, channels), (0, image), 0),
            pl.BlockSpec((None, *kernels.shape[1:]), lambda *_: (0, 0, 0, 0)),
        ],
        out_specs=whole((pixels, channels)),
        scratch_shapes=[pltpu.VMEM((3, pixels + 2 * width, channels), bf16)],
        cost_estimate=cost(pixels, channels, 9, pixels * channels * 12),
        name="section_end",
    )(guess, slopes, kernels)


def stage_kernel(width, factor, first_row, low_row, has_tail, gives_tail, *refs):
    refs = list(refs)
    tail = refs.pop(0) if has_tail else None
    arrived, guess, slope, end, kernel = refs[:5]
    out = refs[5]
    tail_out = refs[6] if gives_tail else None
    field, zs = refs[-2:]
    above = max(first_row - 1, 0)
    kept = (low_row - above) * width
    new = arrived.shape[0]
    if has_tail:
        field[pl.ds(0, kept), :] = tail[...]
    field[pl.ds(kept, new), :] = arrived[...] - guess[...]
    lead = (above - (first_row - 1)) * width
    count = kept + new
    if lead:
        blank(zs, 0, lead)
    fill(zs, lead, slope[...].astype(f32) * field[...], width)
    rest = zs.shape[1] - lead - count
    if rest:
        blank(zs, lead + count, rest)
    base = (first_row - above) * width
    conv_into(
        out, zs, kernel, width,
        lambda s, n, moved: field[pl.ds(base + s, n), :] + factor * moved + end[pl.ds(s, n), :],
    )
    if gives_tail:
        tail_out[...] = field[pl.ds(count - 2 * width, 2 * width), :]


def stage(arrived, tail, guess, slopes, kernels, end, image, factor, rows, width):
    first, low, last, high, height = rows
    layers, _, _, channels = guess.shape
    above = max(first - 1, 0)
    gives_tail = high < height
    count = (last - first) * width
    in_specs = [] if tail is None else [whole(tail.shape)]
    in_specs += [
        whole(arrived.shape),
        window(arrived.shape, (layers - 1, image), low * width),
        window(((high - above) * width, channels), (0, image), above * width),
        window((count, channels), (), first * width),
        pl.BlockSpec((None, *kernels.shape[1:]), lambda *_: (0, 0, 0, 0)),
    ]
    out_shape = [jax.ShapeDtypeStruct((count, channels), f32)]
    if gives_tail:
        out_shape.append(jax.ShapeDtypeStruct((2 * width, channels), f32))
    results = pl.pallas_call(
        functools.partial(stage_kernel, width, factor, first, low, tail is not None, gives_tail),
        out_shape=out_shape,
        grid=(1,),
        in_specs=in_specs,
        out_specs=[whole(s.shape) for s in out_shape],
        scratch_shapes=[
            pltpu.VMEM(((high - above) * width, channels), f32),
            pltpu.VMEM((3, count + 2 * width, channels), bf16),
        ],
        cost_estimate=cost(count, channels, 9, count * channels * 20),
        name="stage",
    )(*(() if tail is None else (tail,)), arrived, guess, slopes, end, kernels)
    return results[0], (results[1] if gives_tail else None)


def grads_into(acc, zs, states, width, scale, before):
    pixels = states.shape[0]
    turned = states[...].T
    for a in range(3):
        for b in range(3):
            rows = zs[b, pl.ds((2 - a) * width, pixels), :]
            term = lax.dot_general(
                turned, rows, (((1,), (0,)), ((), ())), preferred_element_type=f32
            )
            if before is not None:
                term = term + before[3 * a + b]
            acc[3 * a + b] = term * scale if scale != 1.0 else term


def hand_out(acc, side, mine, away, share):
    for node in range(mine.shape[0]):
        base = 2 * node * share
        kept = pl.multiple_of(base + side * share, share)
        sent = pl.multiple_of(base + (1 - side) * share, share)
        mine[node] = acc[:, pl.ds(kept, share), :]
        away[node] = acc[:, pl.ds(sent, share), :]


def top_kernel(width, pieces, final, scale, share, *refs):
    place, *refs = refs
    arrived, refs = refs[:pieces], list(refs[pieces:])
    guess, slope, states = refs[:3]
    del refs[:3]
    before = refs.pop(0) if final else None
    if final:
        adjoint, mine, away, acc, zs = refs
    else:
        adjoint, acc, zs = refs
    pixels = guess.shape[0]
    top = place[0] == 1
    adjoint[...] = jnp.where(top, guess[...], 0.0)
    row = 0
    for ref in arrived:
        count = ref.shape[0]
        spot = pl.ds(row, count)
        adjoint[spot, :] = adjoint[spot, :] + ref[...]
        row = (row + count) % pixels
    blank(zs, 0, width)
    blank(zs, pixels + width, width)
    fill(zs, width, slope[...].astype(f32) * adjoint[...], width)
    grads_into(acc, zs, states, width, scale, before)
    if final:
        hand_out(acc, place[1], mine, away, share)


def top_of(place, arrived, guess, slopes, states, before, image, width, scale, share):
    layers, _, pixels, channels = guess.shape
    final = before is not None
    grad = (9, channels, channels)
    split = (channels // share // 2, 9, share, channels)
    tile = window((pixels, channels), (layers - 1, image), 0)
    in_specs = [pl.BlockSpec(memory_space=pltpu.SMEM)]
    in_specs += [whole(p.shape) for p in arrived] + [tile, tile, tile]
    out_shape = [jax.ShapeDtypeStruct((pixels, channels), f32)]
    scratch = [pltpu.VMEM((3, pixels + 2 * width, channels), bf16)]
    if final:
        in_specs.append(whole(grad))
        out_shape += [jax.ShapeDtypeStruct(split, f32)] * 2
        scratch.insert(0, pltpu.VMEM(grad, f32))
    else:
        out_shape.append(jax.ShapeDtypeStruct(grad, f32))
    return pl.pallas_call(
        functools.partial(top_kernel, width, len(arrived), final, scale, share),
        out_shape=out_shape,
        grid=(1,),
        in_specs=in_specs,
        out_specs=[whole(s.shape) for s in out_shape],
        scratch_shapes=scratch,
        cost_estimate=cost(pixels, channels, 9, pixels * channels * 20),
        name="top",
    )(place, *arrived, guess, slopes, states, *((before,) if final else ()))


def inner_kernel(width, final, scale, share, *refs):
    place, adjoint, slope_above, slope, states, kernel = refs[:6]
    refs = list(refs[6:])
    before = refs.pop(0) if final else None
    if final:
        below, mine, away, acc, zs, zs2 = refs
    else:
        below, acc, zs, zs2 = refs
    pixels = adjoint.shape[0]
    for z in (zs, zs2):
        blank(z, 0, width)
        blank(z, pixels + width, width)
    fill(zs, width, slope_above[...].astype(f32) * adjoint[...], width)
    conv_into(
        below, zs, kernel, width,
        lambda s, n, moved: adjoint[pl.ds(s, n), :] + step_size * moved,
    )
    fill(zs2, width, slope[...].astype(f32) * below[...], width)
    grads_into(acc, zs2, states, width, scale, before)
    if final:
        hand_out(acc, place[1], mine, away, share)


def inner_of(place, adjoint, slopes, states, kernels, before, layer, image, width, scale, share):
    pixels, channels = adjoint.shape
    final = before is not None
    grad = (9, channels, channels)
    split = (channels // share // 2, 9, share, channels)
    in_specs = [
        pl.BlockSpec(memory_space=pltpu.SMEM),
        whole((pixels, channels)),
        window((pixels, channels), (layer + 1, image), 0),
        window((pixels, channels), (layer, image), 0),
        window((pixels, channels), (layer, image), 0),
        pl.BlockSpec((None, *kernels.shape[1:]), lambda *_: (layer + 1, 0, 0, 0)),
    ]
    out_shape = [jax.ShapeDtypeStruct((pixels, channels), f32)]
    scratch = [pltpu.VMEM((3, pixels + 2 * width, channels), bf16)] * 2
    if final:
        in_specs.append(whole(grad))
        out_shape += [jax.ShapeDtypeStruct(split, f32)] * 2
        scratch.insert(0, pltpu.VMEM(grad, f32))
    else:
        out_shape.append(jax.ShapeDtypeStruct(grad, f32))
    return pl.pallas_call(
        functools.partial(inner_kernel, width, final, scale, share),
        out_shape=out_shape,
        grid=(1,),
        in_specs=in_specs,
        out_specs=[whole(s.shape) for s in out_shape],
        scratch_shapes=scratch,
        cost_estimate=cost(pixels, channels, 18, pixels * channels * 20),
        name="inner",
    )(place, adjoint, slopes, slopes, states, kernels, *((before,) if final else ()))


def lower_kernel(width, *refs):
    first, second, slope, kernel, out, zs = refs
    pixels = first.shape[0]
    for image, adjoint in enumerate((first, second)):
        blank(zs, 0, width)
        blank(zs, pixels + width, width)
        fill(zs, width, slope[image].astype(f32) * adjoint[...], width)
        conv_into(
            out.at[image], zs, kernel, width,
            lambda s, n, moved, adjoint=adjoint: adjoint[pl.ds(s, n), :] + step_size * moved,
        )


def lower_of(adjoints, slopes, kernels, width):
    images = len(adjoints)
    pixels, channels = adjoints[0].shape
    return pl.pallas_call(
        functools.partial(lower_kernel, width),
        out_shape=jax.ShapeDtypeStruct((images, pixels, channels), f32),
        grid=(1,),
        in_specs=[whole((pixels, channels))] * images
        + [
            pl.BlockSpec((None, images, pixels, channels), lambda *_: (0, 0, 0, 0)),
            pl.BlockSpec((None, *kernels.shape[1:]), lambda *_: (0, 0, 0, 0)),
        ],
        out_specs=whole((images, pixels, channels)),
        scratch_shapes=[pltpu.VMEM((3, pixels + 2 * width, channels), bf16)],
        cost_estimate=cost(images * pixels, channels, 9, images * pixels * channels * 12),
        name="lower",
    )(*adjoints, slopes, kernels)


def cuts_of(height, hops):
    piece = height // PIECES
    return [
        [0] + [min(height, piece * (k + 1) + hops - 1 - hop) for k in range(PIECES - 1)] + [height]
        for hop in range(hops)
    ]


def chain(ends, guess, slopes, kernels, factor, width):
    sections = lax.axis_size("layer")
    images, pixels, channels = len(ends), *ends[0].shape
    height = pixels // width
    hops = sections - 1
    cuts = cuts_of(height, hops)
    payload = [
        [ends[i][low * width : high * width] for low, high in zip(cuts[0], cuts[0][1:])]
        for i in range(images)
    ]
    arrivals = []
    for hop in range(hops):
        pairs = [(sections - 1 - hop, sections - 2 - hop)]
        following, here = [], []
        for i in range(images):
            sent, got, tail = [], [], None
            for k, rows in enumerate(payload[i]):
                arrived = lax.ppermute(rows, "layer", pairs)
                got.append(arrived)
                if hop + 1 < hops:
                    low, high = cuts[hop][k : k + 2]
                    first, last = cuts[hop + 1][k : k + 2]
                    passed, tail = stage(
                        arrived, tail, guess, slopes, kernels, ends[i], i, factor,
                        (first, low, last, high, height), width,
                    )
                    sent.append(passed)
            following.append(sent)
            here.append(got)
        arrivals.append(here)
        payload = following
    return arrivals


def scatter_sum(mine, away):
    replicas = lax.axis_size("dp")
    node = lax.axis_index("dp") // 2
    nodes = replicas // 2
    got = lax.ppermute(away, "dp", [(i, i ^ 1) for i in range(replicas)])
    held = mine + got

    def block(index):
        return lax.dynamic_index_in_dim(held, jnp.clip(index, 0, nodes - 1), 0, keepdims=False)

    total = block(node)
    up = down = None
    for tick in range(1, nodes):
        up_out, down_out = block(node + nodes - tick), block(node - nodes + tick)
        if up is not None:
            up_out, down_out = up_out + up, down_out + down
        up_pairs = [(2 * n + s, 2 * n + 2 + s) for n in range(tick) for s in range(2)]
        down_pairs = [
            (2 * n + s, 2 * n - 2 + s) for n in range(nodes - tick, nodes) for s in range(2)
        ]
        up = lax.ppermute(up_out, "dp", up_pairs)
        down = lax.ppermute(down_out, "dp", down_pairs)
    return total + up + down


def on_device(states, slopes, kernels, guess):
    layers, images, height, width, channels = states.shape
    flat = (layers, images, height * width, channels)
    states, slopes, guess = (x.reshape(flat) for x in (states, slopes, guess))
    replicas = lax.axis_size("dp")
    sections = lax.axis_size("layer")
    share = channels // replicas
    place = jnp.stack(
        [
            (lax.axis_index("layer") == sections - 1).astype(jnp.int32),
            (lax.axis_index("dp") % 2).astype(jnp.int32),
        ]
    )
    ends = [section_end_of(guess, slopes, kernels, i, width) for i in range(images)]
    arrivals = chain(ends, guess, slopes, kernels, step_size * layers, width)
    scale = step_size / (images * replicas)
    adjoints = [None] * images
    partial = None
    for i in range(images):
        final = i == images - 1
        pieces = [p for hop in arrivals for p in hop[i]]
        adjoints[i], *partial = top_of(
            place, pieces, guess, slopes, states, partial[0] if final else None, i, width,
            scale if final else 1.0, share,
        )
    gradients = [None] * layers
    gradients[layers - 1] = scatter_sum(*partial)
    for layer in range(layers - 2, -1, -1):
        partial = None
        for i in range(images):
            final = i == images - 1
            adjoints[i], *partial = inner_of(
                place, adjoints[i], slopes, states, kernels, partial[0] if final else None,
                layer, i, width, scale if final else 1.0, share,
            )
        gradients[layer] = scatter_sum(*partial)
    lower = lower_of(adjoints, slopes, kernels, width)
    return lower.reshape(1, images, height, width, channels), jnp.stack(gradients)


def solution(mesh):
    return jax.shard_map(
        on_device,
        mesh=mesh,
        in_specs=(
            P("layer", "dp", None, None, None),
            P("layer", "dp", None, None, None),
            P("layer", None, None, None),
            P("layer", "dp", None, None, None),
        ),
        out_specs=(P("layer", "dp", None, None, None), P("layer", None, "dp", None)),
        check_vma=False,
    )
```

```python
import functools

import jax
import jax.numpy as jnp
from jax import lax
from jax.experimental import pallas as pl
from jax.experimental.pallas import tpu as pltpu
from jax.sharding import PartitionSpec as P


PIECES = 4

step_size = 0.5

f32 = jnp.float32
bf16 = jnp.bfloat16


def tile_of(size):
    if size <= 384:
        return size
    for tile in (256, 128, 64, 32):
        if size % tile == 0:
            return tile
    return size


def limits(megabytes):
    return pltpu.CompilerParams(vmem_limit_bytes=megabytes << 20)


def fill(zs, first, z, width):
    count = z.shape[0]
    column = lax.broadcasted_iota(jnp.int32, z.shape, 0) % width
    after = jnp.where(column == width - 1, 0.0, pltpu.roll(z, count - 1, 0))
    before = jnp.where(column == 0, 0.0, pltpu.roll(z, 1, 0))
    rows = pl.ds(first, count)
    zs[0, rows, :] = after.astype(bf16)
    zs[1, rows, :] = z.astype(bf16)
    zs[2, rows, :] = before.astype(bf16)


def blank(zs, first, count):
    zs[:, pl.ds(first, count), :] = jnp.zeros((3, count, zs.shape[2]), bf16)


def taps_at(zs, kernel_ref, start, size, width):
    total = None
    for a in range(3):
        for b in range(3):
            rows = zs[b, pl.ds(start + (2 - a) * width, size), :]
            term = lax.dot_general(
                rows, kernel_ref[3 * a + b], (((1,), (1,)), ((), ())), preferred_element_type=f32
            )
            total = term if total is None else total + term
    return total


def conv_into(out, zs, kernel_ref, width, finish):
    for start, tile in tiles_of(out.shape[0]):
        out[pl.ds(start, tile), :] = finish(start, tile, taps_at(zs, kernel_ref, start, tile, width))


def window(shape, lead, first):
    spec = (None,) * len(lead) + (pl.Element(shape[0]), pl.Element(shape[1]))
    return pl.BlockSpec(spec, lambda *_: (*lead, first, 0))


def cost(rows, channels, taps, moved):
    return pl.CostEstimate(
        flops=2 * rows * channels * channels * taps, bytes_accessed=moved, transcendentals=0
    )


def whole(shape):
    return pl.BlockSpec(shape, lambda *_: (0,) * len(shape))


def end_kernel(width, first_row, low_row, counts, *refs):
    guess, slope, kernel = refs[:3]
    outs, (zs,) = refs[-1 - len(counts) : -1], refs[-1:]
    lead = (first_row - (low_row - 1)) * width
    count = guess.shape[0]
    if lead:
        blank(zs, 0, lead)
    fill(zs, lead, slope[...].astype(f32) * guess[...], width)
    rest = zs.shape[1] - lead - count
    if rest:
        blank(zs, lead + count, rest)
    base = 0
    inside = (low_row - first_row) * width
    for out in outs:
        for start, size in tiles_of(out.shape[0]):
            moved = taps_at(zs, kernel, base + start, size, width)
            rows = pl.ds(inside + base + start, size)
            out[pl.ds(start, size), :] = guess[rows, :] + step_size * moved
        base += out.shape[0]


def tiles_of(count):
    tile = tile_of(count)
    return [(start, tile) for start in range(0, count, tile)]


def section_end_of(guess, slopes, kernels, image, cuts, width, after):
    pixels, channels = guess.shape[2:]
    height = pixels // width
    low, high = cuts[0], cuts[-1]
    first, last = max(low - 1, 0), min(high + 1, height)
    rows = window(((last - first) * width, channels), (0, image), first * width)
    shapes = [((b - a) * width, channels) for a, b in zip(cuts, cuts[1:])]
    anywhere = [pl.BlockSpec(memory_space=pl.ANY)] * len(after)
    return pl.pallas_call(
        functools.partial(end_kernel, width, first, low, shapes),
        out_shape=[jax.ShapeDtypeStruct(s, f32) for s in shapes],
        grid=(1,),
        in_specs=[rows, rows, pl.BlockSpec((None, *kernels.shape[1:]), lambda *_: (0, 0, 0, 0))]
        + anywhere,
        out_specs=[whole(s) for s in shapes],
        scratch_shapes=[pltpu.VMEM((3, (high - low + 2) * width, channels), bf16)],
        cost_estimate=cost((high - low) * width, channels, 9, (high - low) * width * channels * 12),
        compiler_params=limits(16) if after else None,
        name="section_end",
    )(guess, slopes, kernels, *after)


def stage_kernel(width, factor, first_row, low_row, has_tail, gives_tail, spans, owner, *refs):
    place, *refs = refs
    tail = refs.pop(0) if has_tail else None
    arrived, guess, slope, kernel = refs[:4]
    ends = refs[4 : 4 + len(spans)]
    out = refs[4 + len(spans)]
    tail_out = refs[5 + len(spans)] if gives_tail else None
    field, zs = refs[-2:]
    above = max(first_row - 1, 0)
    kept = (low_row - above) * width
    new = arrived.shape[0]

    @pl.when(place[0] == owner)
    def _():
        if has_tail:
            field[pl.ds(0, kept), :] = tail[...]
        field[pl.ds(kept, new), :] = arrived[...] - guess[...]
        lead = (above - (first_row - 1)) * width
        count = kept + new
        if lead:
            blank(zs, 0, lead)
        fill(zs, lead, slope[...].astype(f32) * field[...], width)
        rest = zs.shape[1] - lead - count
        if rest:
            blank(zs, lead + count, rest)
        if gives_tail:
            tail_out[...] = field[pl.ds(count - 2 * width, 2 * width), :]
        base = (first_row - above) * width
        for start, size in tiles_of(out.shape[0]):
            moved = taps_at(zs, kernel, start, size, width)
            out[pl.ds(start, size), :] = field[pl.ds(base + start, size), :] + factor * moved
        for (top, begin, size), end in zip(spans, ends):
            rows = pl.ds(top, size)
            out[rows, :] = out[rows, :] + end[pl.ds(begin, size), :]


def stage(place, owner, arrived, tail, guess, slopes, kernels, ends, image, factor, rows, width):
    first, low, last, high, height = rows
    layers, _, _, channels = guess.shape
    above = max(first - 1, 0)
    gives_tail = high < height
    count = (last - first) * width
    used, spans = [], []
    for begin, piece in ends:
        stop = begin + piece.shape[0] // width
        a, b = max(begin, first), min(stop, last)
        if a < b:
            used.append(piece)
            spans.append(((a - first) * width, (a - begin) * width, (b - a) * width))
    in_specs = [pl.BlockSpec(memory_space=pltpu.SMEM)]
    in_specs += [] if tail is None else [whole(tail.shape)]
    in_specs += [
        whole(arrived.shape),
        window(arrived.shape, (layers - 1, image), low * width),
        window(((high - above) * width, channels), (0, image), above * width),
        pl.BlockSpec((None, *kernels.shape[1:]), lambda *_: (0, 0, 0, 0)),
    ] + [whole(piece.shape) for piece in used]
    out_shape = [jax.ShapeDtypeStruct((count, channels), f32)]
    if gives_tail:
        out_shape.append(jax.ShapeDtypeStruct((2 * width, channels), f32))
    results = pl.pallas_call(
        functools.partial(
            stage_kernel, width, factor, first, low, tail is not None, gives_tail,
            spans, owner,
        ),
        out_shape=out_shape,
        grid=(1,),
        in_specs=in_specs,
        out_specs=[whole(s.shape) for s in out_shape],
        scratch_shapes=[
            pltpu.VMEM(((high - above) * width, channels), f32),
            pltpu.VMEM((3, count + 2 * width, channels), bf16),
        ],
        cost_estimate=cost(count, channels, 9, count * channels * 20),
        compiler_params=limits(12),
        name="stage",
    )(place, *(() if tail is None else (tail,)), arrived, guess, slopes, kernels, *used)
    return results[0], (results[1] if gives_tail else None)


def grads_into(acc, zs, states, width, scale, before):
    pixels = states.shape[0]
    turned = states[...].T
    for a in range(3):
        for b in range(3):
            rows = zs[b, pl.ds((2 - a) * width, pixels), :]
            term = lax.dot_general(
                turned, rows, (((1,), (0,)), ((), ())), preferred_element_type=f32
            )
            if before is not None:
                term = term + before[3 * a + b]
            acc[3 * a + b] = term * scale if scale != 1.0 else term


def hand_out(acc, side, mine, away, share):
    for node in range(mine.shape[0]):
        base = 2 * node * share
        kept = pl.multiple_of(base + side * share, share)
        sent = pl.multiple_of(base + (1 - side) * share, share)
        mine[node] = acc[:, pl.ds(kept, share), :]
        away[node] = acc[:, pl.ds(sent, share), :]


def top_kernel(width, hops, final, scale, share, *refs):
    place, *refs = refs
    arrived = []
    for pieces in hops:
        arrived.append(refs[:pieces])
        refs = refs[pieces:]
    guess, slope, states = refs[:3]
    refs = refs[3:]
    if final:
        before, _, adjoint, mine, away, acc, zs = refs
    else:
        before = None
        adjoint, acc, zs = refs
    pixels = guess.shape[0]

    @pl.when(place[0] == len(hops))
    def _():
        adjoint[...] = guess[...]

    for hop, pieces in enumerate(arrived):

        @pl.when(place[0] == len(hops) - 1 - hop)
        def _(pieces=pieces):
            row = 0
            for piece in pieces:
                adjoint[pl.ds(row, piece.shape[0]), :] = piece[...]
                row += piece.shape[0]

    blank(zs, 0, width)
    blank(zs, pixels + width, width)
    fill(zs, width, slope[...].astype(f32) * adjoint[...], width)
    grads_into(acc, zs, states, width, scale, before)
    if final:
        hand_out(acc, place[1], mine, away, share)


def top_of(place, arrived, guess, slopes, states, before, after, image, width, scale, share):
    layers, _, pixels, channels = guess.shape
    final = before is not None
    grad = (9, channels, channels)
    split = (channels // share // 2, 9, share, channels)
    tile = window((pixels, channels), (layers - 1, image), 0)
    pieces = [p for hop in arrived for p in hop]
    in_specs = [pl.BlockSpec(memory_space=pltpu.SMEM)]
    in_specs += [whole(p.shape) for p in pieces] + [tile, tile, tile]
    out_shape = [jax.ShapeDtypeStruct((pixels, channels), f32)]
    scratch = [pltpu.VMEM((3, pixels + 2 * width, channels), bf16)]
    if final:
        in_specs += [whole(grad), pl.BlockSpec(memory_space=pl.ANY)]
        out_shape += [jax.ShapeDtypeStruct(split, f32)] * 2
        scratch.insert(0, pltpu.VMEM(grad, f32))
    else:
        out_shape.append(jax.ShapeDtypeStruct(grad, f32))
    return pl.pallas_call(
        functools.partial(top_kernel, width, [len(hop) for hop in arrived], final, scale, share),
        out_shape=out_shape,
        grid=(1,),
        in_specs=in_specs,
        out_specs=[whole(s.shape) for s in out_shape],
        scratch_shapes=scratch,
        cost_estimate=cost(pixels, channels, 9, pixels * channels * 20),
        compiler_params=limits(36),
        name="top",
    )(place, *pieces, guess, slopes, states, *((before, after) if final else ()))


def inner_kernel(width, final, scale, share, *refs):
    place, adjoint, slope_above, slope, states, kernel = refs[:6]
    refs = list(refs[6:])
    before = refs.pop(0) if final else None
    if final:
        below, mine, away, acc, zs, zs2 = refs
    else:
        below, acc, zs, zs2 = refs
    pixels = adjoint.shape[0]
    for z in (zs, zs2):
        blank(z, 0, width)
        blank(z, pixels + width, width)
    fill(zs, width, slope_above[...].astype(f32) * adjoint[...], width)
    conv_into(
        below, zs, kernel, width,
        lambda s, n, moved: adjoint[pl.ds(s, n), :] + step_size * moved,
    )
    fill(zs2, width, slope[...].astype(f32) * below[...], width)
    grads_into(acc, zs2, states, width, scale, before)
    if final:
        hand_out(acc, place[1], mine, away, share)


def inner_of(place, adjoint, slopes, states, kernels, before, layer, image, width, scale, share):
    pixels, channels = adjoint.shape
    final = before is not None
    grad = (9, channels, channels)
    split = (channels // share // 2, 9, share, channels)
    in_specs = [
        pl.BlockSpec(memory_space=pltpu.SMEM),
        whole((pixels, channels)),
        window((pixels, channels), (layer + 1, image), 0),
        window((pixels, channels), (layer, image), 0),
        window((pixels, channels), (layer, image), 0),
        pl.BlockSpec((None, *kernels.shape[1:]), lambda *_: (layer + 1, 0, 0, 0)),
    ]
    out_shape = [jax.ShapeDtypeStruct((pixels, channels), f32)]
    scratch = [pltpu.VMEM((3, pixels + 2 * width, channels), bf16)] * 2
    if final:
        in_specs.append(whole(grad))
        out_shape += [jax.ShapeDtypeStruct(split, f32)] * 2
        scratch.insert(0, pltpu.VMEM(grad, f32))
    else:
        out_shape.append(jax.ShapeDtypeStruct(grad, f32))
    return pl.pallas_call(
        functools.partial(inner_kernel, width, final, scale, share),
        out_shape=out_shape,
        grid=(1,),
        in_specs=in_specs,
        out_specs=[whole(s.shape) for s in out_shape],
        scratch_shapes=scratch,
        cost_estimate=cost(pixels, channels, 18, pixels * channels * 20),
        compiler_params=limits(36),
        name="inner",
    )(place, adjoint, slopes, slopes, states, kernels, *((before,) if final else ()))


def lower_kernel(width, adjoint, slope, kernel, *refs):
    out, zs = refs[-2:]
    pixels = adjoint.shape[0]
    blank(zs, 0, width)
    blank(zs, pixels + width, width)
    fill(zs, width, slope[...].astype(f32) * adjoint[...], width)
    conv_into(
        out, zs, kernel, width,
        lambda s, n, moved: adjoint[pl.ds(s, n), :] + step_size * moved,
    )


def lower_of(adjoint, slopes, kernels, image, images, into, width):
    pixels, channels = adjoint.shape
    return pl.pallas_call(
        functools.partial(lower_kernel, width),
        out_shape=jax.ShapeDtypeStruct((images, pixels, channels), f32),
        grid=(1,),
        in_specs=[
            whole((pixels, channels)),
            window((pixels, channels), (0, image), 0),
            pl.BlockSpec((None, *kernels.shape[1:]), lambda *_: (0, 0, 0, 0)),
        ]
        + [pl.BlockSpec(memory_space=pl.ANY)] * len(into),
        out_specs=pl.BlockSpec((None, pixels, channels), lambda *_: (image, 0, 0)),
        scratch_shapes=[pltpu.VMEM((3, pixels + 2 * width, channels), bf16)],
        input_output_aliases={3: 0} if into else {},
        cost_estimate=cost(pixels, channels, 9, pixels * channels * 12),
        compiler_params=limits(16),
        name="lower",
    )(adjoint, slopes, kernels, *into)


def cuts_of(height, hops):
    piece = height // PIECES
    return [
        [0] + [min(height, piece * (k + 1) + hops - 1 - hop) for k in range(PIECES - 1)] + [height]
        for hop in range(hops)
    ]


def chain(place, ends, cuts, guess, slopes, kernels, factor, width):
    sections = lax.axis_size("layer")
    images, pixels = guess.shape[1:3]
    height = pixels // width
    hops = sections - 1
    payload = ends
    arrivals = [[] for _ in range(images)]
    for hop in range(hops):
        pairs = [(sections - 1 - hop, sections - 2 - hop)]
        following = []
        for i in range(images):
            sent, got, tail = [], [], None
            for k, rows in enumerate(payload[i]):
                arrived = lax.ppermute(rows, "layer", pairs)
                got.append(arrived)
                if hop + 1 < hops:
                    low, high = cuts[hop][k : k + 2]
                    first, last = cuts[hop + 1][k : k + 2]
                    passed, tail = stage(
                        place, sections - 2 - hop, arrived, tail, guess, slopes, kernels,
                        list(zip(cuts[0], ends[i])), i, factor,
                        (first, low, last, high, height), width,
                    )
                    sent.append(passed)
            following.append(sent)
            arrivals[i].append(got)
        payload = following
    return arrivals


def both_sides(pairs):
    return [(2 * a + side, 2 * b + side) for a, b in pairs for side in range(2)]


def join_kernel(place, mine, got, held, *outs):
    held[...] = mine[...] + got[...]
    last = held.shape[0] - 1
    for item, out in enumerate(outs):
        out[...] = held[jnp.where(place[2] == 0, last - item, item)]


def join(place, mine, got):
    nodes, *block = mine.shape
    shapes = [mine.shape] + [tuple(block)] * (nodes - 1)
    return pl.pallas_call(
        join_kernel,
        out_shape=[jax.ShapeDtypeStruct(x, f32) for x in shapes],
        grid=(1,),
        in_specs=[pl.BlockSpec(memory_space=pltpu.SMEM)] + [whole(mine.shape)] * 2,
        out_specs=[whole(x) for x in shapes],
        cost_estimate=pl.CostEstimate(flops=mine.size, bytes_accessed=16 * mine.size, transcendentals=0),
        compiler_params=limits(16),
        name="join",
    )(place, mine, got)


def relay_kernel(place, held, arrived, out):
    out[...] = held[...] + arrived[...]


def relay(place, held, arrived, wave, item):
    last = held.shape[0] - 1
    block = held.shape[1:]

    def which(_, place):
        return (jnp.where(place[2] == wave - 1, last - item, item), 0, 0, 0)

    return pl.pallas_call(
        relay_kernel,
        out_shape=jax.ShapeDtypeStruct(block, f32),
        grid_spec=pltpu.PrefetchScalarGridSpec(
            num_scalar_prefetch=1,
            grid=(1,),
            in_specs=[pl.BlockSpec((None, *block), which), whole(block)],
            out_specs=whole(block),
        ),
        cost_estimate=pl.CostEstimate(
            flops=arrived.size, bytes_accessed=12 * arrived.size, transcendentals=0
        ),
        compiler_params=limits(12),
        name="relay",
    )(place, held, arrived)


def total_kernel(nodes, place, held, *refs):
    arrived, out = refs[: nodes - 1], refs[-1]
    out[...] = held[...]
    for wave, piece in enumerate(arrived, 1):

        @pl.when((place[2] == wave) | (place[2] == nodes - 1 - wave))
        def _(piece=piece):
            out[...] = out[...] + piece[...]


def total(place, held, arrived, layer, layers, into):
    nodes, *block = held.shape
    return pl.pallas_call(
        functools.partial(total_kernel, nodes),
        out_shape=jax.ShapeDtypeStruct((layers, *block), f32),
        grid_spec=pltpu.PrefetchScalarGridSpec(
            num_scalar_prefetch=1,
            grid=(1,),
            in_specs=[pl.BlockSpec((None, *block), lambda _, place: (place[2], 0, 0, 0))]
            + [whole(tuple(block))] * len(arrived)
            + [pl.BlockSpec(memory_space=pl.ANY)] * len(into),
            out_specs=pl.BlockSpec((None, *block), lambda *_: (layer, 0, 0, 0)),
        ),
        input_output_aliases={2 + len(arrived): 0} if into else {},
        cost_estimate=pl.CostEstimate(
            flops=held.size, bytes_accessed=4 * held.size, transcendentals=0
        ),
        compiler_params=limits(12),
        name="total",
    )(place, held, *arrived, *into)


def line_sum(place, mine, away, layer, layers, into):
    replicas = lax.axis_size("dp")
    nodes = replicas // 2
    got = lax.ppermute(away, "dp", [(i, i ^ 1) for i in range(replicas)])
    held, *sends = join(place, mine, got)
    arrived = {}
    for wave in range(1, nodes):
        pairs = both_sides([(wave - 1, wave), (nodes - wave, nodes - 1 - wave)])
        for item in range(nodes - wave):
            out = sends[item]
            if wave > 1:
                out = relay(place, held, arrived[wave - 1, item], wave, item)
            arrived[wave, item] = lax.ppermute(out, "dp", pairs)
    last = [arrived[wave, nodes - 1 - wave] for wave in range(1, nodes)]
    return total(place, held, last, layer, layers, into)


def plain_sum(mine, away):
    nodes, taps, share, channels = mine.shape
    side = lax.axis_index("dp") % 2
    first, second = jnp.where(side == 0, mine, away), jnp.where(side == 0, away, mine)
    terms = jnp.stack([first, second], axis=1).reshape(2 * nodes, taps, share, channels)
    return lax.psum_scatter(terms, "dp", scatter_dimension=0, tiled=False)


def on_device(states, slopes, kernels, guess):
    layers, images, height, width, channels = states.shape
    flat = (layers, images, height * width, channels)
    states, slopes, guess = (x.reshape(flat) for x in (states, slopes, guess))
    replicas = lax.axis_size("dp")
    sections = lax.axis_size("layer")
    share = channels // replicas
    device = lax.axis_index("dp")
    place = jnp.stack([lax.axis_index("layer"), device % 2, device // 2]).astype(jnp.int32)
    cuts = cuts_of(height, sections - 1)
    ends = [section_end_of(guess, slopes, kernels, 0, cuts[0][:2], width, ())]
    ends[0] += section_end_of(guess, slopes, kernels, 0, cuts[0][1:], width, ends[0])
    for i in range(1, images):
        ends.append(section_end_of(guess, slopes, kernels, i, cuts[0], width, ends[i - 1][-1:]))
    arrivals = chain(place, ends, cuts, guess, slopes, kernels, step_size * layers, width)
    scale = step_size / (images * replicas)
    adjoints = [None] * images
    grads = [None] * layers
    for i in range(images):
        final = i == images - 1
        for layer in range(layers - 1, -1, -1):
            if layer == layers - 1:
                adjoints[i], *grads[layer] = top_of(
                    place, arrivals[i], guess, slopes, states,
                    grads[layer][0] if final else None, adjoints[i - 1] if final else None, i,
                    width, scale if final else 1.0, share,
                )
            else:
                adjoints[i], *grads[layer] = inner_of(
                    place, adjoints[i], slopes, states, kernels,
                    grads[layer][0] if final else None, layer, i, width,
                    scale if final else 1.0, share,
                )
    lower = ()
    for i in range(images):
        lower = (lower_of(adjoints[i], slopes, kernels, i, images, lower, width),)
    if replicas in (4, 8):
        gradients = ()
        for layer in range(layers - 1, -1, -1):
            gradients = (line_sum(place, *grads[layer], layer, layers, gradients),)
        gradients = gradients[0]
    else:
        gradients = jnp.stack([plain_sum(*grads[layer]) for layer in range(layers)])
    return lower[0].reshape(1, images, height, width, channels), gradients


def solution(mesh):
    return jax.shard_map(
        on_device,
        mesh=mesh,
        in_specs=(
            P("layer", "dp", None, None, None),
            P("layer", "dp", None, None, None),
            P("layer", None, None, None),
            P("layer", "dp", None, None, None),
        ),
        out_specs=(P("layer", "dp", None, None, None), P("layer", None, "dp", None)),
        check_vma=False,
    )
```

```python
import functools

import jax
import jax.numpy as jnp
from jax import lax
from jax.experimental import pallas as pl
from jax.experimental.pallas import tpu as pltpu
from jax.sharding import PartitionSpec as P


PIECES = 4

step_size = 0.5

f32 = jnp.float32
bf16 = jnp.bfloat16


def tile_of(size):
    if size <= 384:
        return size
    for tile in (256, 128, 64, 32):
        if size % tile == 0:
            return tile
    return size


def limits(megabytes):
    return pltpu.CompilerParams(vmem_limit_bytes=megabytes << 20)


def fill(zs, first, z, width):
    count = z.shape[0]
    column = lax.broadcasted_iota(jnp.int32, z.shape, 0) % width
    after = jnp.where(column == width - 1, 0.0, pltpu.roll(z, count - 1, 0))
    before = jnp.where(column == 0, 0.0, pltpu.roll(z, 1, 0))
    rows = pl.ds(first, count)
    zs[0, rows, :] = after.astype(bf16)
    zs[1, rows, :] = z.astype(bf16)
    zs[2, rows, :] = before.astype(bf16)


def blank(zs, first, count):
    zs[:, pl.ds(first, count), :] = jnp.zeros((3, count, zs.shape[2]), bf16)


def taps_at(zs, kernel_ref, start, size, width):
    total = None
    for a in range(3):
        for b in range(3):
            rows = zs[b, pl.ds(start + (2 - a) * width, size), :]
            term = lax.dot_general(
                rows, kernel_ref[3 * a + b], (((1,), (1,)), ((), ())), preferred_element_type=f32
            )
            total = term if total is None else total + term
    return total


def conv_into(out, zs, kernel_ref, width, finish):
    for start, tile in tiles_of(out.shape[0]):
        out[pl.ds(start, tile), :] = finish(start, tile, taps_at(zs, kernel_ref, start, tile, width))


def window(shape, lead, first):
    spec = (None,) * len(lead) + (pl.Element(shape[0]), pl.Element(shape[1]))
    return pl.BlockSpec(spec, lambda *_: (*lead, first, 0))


def cost(rows, channels, taps, moved):
    return pl.CostEstimate(
        flops=2 * rows * channels * channels * taps, bytes_accessed=moved, transcendentals=0
    )


def whole(shape):
    return pl.BlockSpec(shape, lambda *_: (0,) * len(shape))


def end_kernel(width, first_row, low_row, counts, extra, copies, *refs):
    guess, slope, kernel = refs[:3]
    outs, zs = refs[3 + extra : -1], refs[-1]
    lead = (first_row - (low_row - 1)) * width
    count = guess.shape[0]
    if lead:
        blank(zs, 0, lead)
    fill(zs, lead, slope[...].astype(f32) * guess[...], width)
    rest = zs.shape[1] - lead - count
    if rest:
        blank(zs, lead + count, rest)
    base = 0
    inside = (low_row - first_row) * width
    for out in outs[: len(counts)]:
        for start, size in tiles_of(out.shape[0]):
            moved = taps_at(zs, kernel, base + start, size, width)
            rows = pl.ds(inside + base + start, size)
            out[pl.ds(start, size), :] = guess[rows, :] + step_size * moved
        base += out.shape[0]
    for source, out in zip(copies, outs[len(counts) :]):
        out[...] = refs[source][...]


def tiles_of(count):
    tile = tile_of(count)
    return [(start, tile) for start in range(0, count, tile)]


def in_hbm(x):
    return pltpu.with_memory_space_constraint(x, pltpu.HBM)


def section_end_of(guess, slopes, kernel, image, cuts, width, keep):
    layers, _, pixels, channels = guess.shape
    height = pixels // width
    low, high = cuts[0], cuts[-1]
    first, last = max(low - 1, 0), min(high + 1, height)
    rows = window(((last - first) * width, channels), (0, image), first * width)
    shapes = [((b - a) * width, channels) for a, b in zip(cuts, cuts[1:])]
    taps = kernel.shape[-3:]
    kernel_spec = whole(taps)
    if kernel.ndim == 4:
        kernel, kernel_spec = in_hbm(kernel), pl.BlockSpec((None, *taps), lambda *_: (0, 0, 0, 0))
    args, in_specs = [in_hbm(guess), in_hbm(slopes), kernel], [rows, rows, kernel_spec]
    out_shape = [jax.ShapeDtypeStruct(x, f32) for x in shapes]
    copies = []
    if keep:
        args += [in_hbm(guess), in_hbm(slopes)]
        in_specs += [window((pixels, channels), (layers - 1, image), 0)]
        in_specs += [window((pixels, channels), (0, image), 0)]
        out_shape += [jax.ShapeDtypeStruct((pixels, channels), t) for t in (f32, slopes.dtype)]
        copies = [3, 4]
        if kernel.ndim == 4:
            out_shape.append(jax.ShapeDtypeStruct(taps, kernel.dtype))
            copies.append(2)
    return pl.pallas_call(
        functools.partial(end_kernel, width, first, low, shapes, len(args) - 3, copies),
        out_shape=out_shape,
        grid=(1,),
        in_specs=in_specs,
        out_specs=[whole(x.shape) for x in out_shape],
        scratch_shapes=[pltpu.VMEM((3, (high - low + 2) * width, channels), bf16)],
        cost_estimate=cost((high - low) * width, channels, 9, (high - low) * width * channels * 12),
        compiler_params=limits(24),
        name="section_end",
    )(*args)


def stage_kernel(width, factor, first_row, low_row, has_tail, gives_tail, spans, owner, *refs):
    place, *refs = refs
    tail = refs.pop(0) if has_tail else None
    arrived, guess, slope, kernel = refs[:4]
    ends = refs[4 : 4 + len(spans)]
    out = refs[4 + len(spans)]
    tail_out = refs[5 + len(spans)] if gives_tail else None
    field, zs = refs[-2:]
    above = max(first_row - 1, 0)
    kept = (low_row - above) * width
    new = arrived.shape[0]

    @pl.when(place[0] == owner)
    def _():
        if has_tail:
            field[pl.ds(0, kept), :] = tail[...]
        field[pl.ds(kept, new), :] = arrived[...] - guess[...]
        lead = (above - (first_row - 1)) * width
        count = kept + new
        if lead:
            blank(zs, 0, lead)
        fill(zs, lead, slope[...].astype(f32) * field[...], width)
        rest = zs.shape[1] - lead - count
        if rest:
            blank(zs, lead + count, rest)
        if gives_tail:
            tail_out[...] = field[pl.ds(count - 2 * width, 2 * width), :]
        base = (first_row - above) * width
        for start, size in tiles_of(out.shape[0]):
            moved = taps_at(zs, kernel, start, size, width)
            out[pl.ds(start, size), :] = field[pl.ds(base + start, size), :] + factor * moved
        for (top, begin, size), end in zip(spans, ends):
            rows = pl.ds(top, size)
            out[rows, :] = out[rows, :] + end[pl.ds(begin, size), :]


def stage(place, owner, arrived, tail, guess, slope, kernel, ends, factor, rows, width):
    first, low, last, high, height = rows
    channels = guess.shape[1]
    above = max(first - 1, 0)
    gives_tail = high < height
    count = (last - first) * width
    used, spans = [], []
    for begin, piece in ends:
        stop = begin + piece.shape[0] // width
        a, b = max(begin, first), min(stop, last)
        if a < b:
            used.append(piece)
            spans.append(((a - first) * width, (a - begin) * width, (b - a) * width))
    in_specs = [pl.BlockSpec(memory_space=pltpu.SMEM)]
    in_specs += [] if tail is None else [whole(tail.shape)]
    in_specs += [
        whole(arrived.shape),
        window(arrived.shape, (), low * width),
        window(((high - above) * width, channels), (), above * width),
        whole(kernel.shape),
    ] + [whole(piece.shape) for piece in used]
    out_shape = [jax.ShapeDtypeStruct((count, channels), f32)]
    if gives_tail:
        out_shape.append(jax.ShapeDtypeStruct((2 * width, channels), f32))
    results = pl.pallas_call(
        functools.partial(
            stage_kernel, width, factor, first, low, tail is not None, gives_tail,
            spans, owner,
        ),
        out_shape=out_shape,
        grid=(1,),
        in_specs=in_specs,
        out_specs=[whole(s.shape) for s in out_shape],
        scratch_shapes=[
            pltpu.VMEM(((high - above) * width, channels), f32),
            pltpu.VMEM((3, count + 2 * width, channels), bf16),
        ],
        cost_estimate=cost(count, channels, 9, count * channels * 20),
        compiler_params=limits(12),
        name="stage",
    )(place, *(() if tail is None else (tail,)), arrived, guess, slope, kernel, *used)
    return results[0], (results[1] if gives_tail else None)


def grads_into(acc, zs, states, width, scale, before):
    pixels = states.shape[0]
    turned = states[...].T
    for a in range(3):
        for b in range(3):
            rows = zs[b, pl.ds((2 - a) * width, pixels), :]
            term = lax.dot_general(
                turned, rows, (((1,), (0,)), ((), ())), preferred_element_type=f32
            )
            if before is not None:
                term = term + before[3 * a + b]
            acc[3 * a + b] = term * scale if scale != 1.0 else term


def hand_out(acc, side, mine, away, share):
    for node in range(mine.shape[0]):
        base = 2 * node * share
        kept = pl.multiple_of(base + side * share, share)
        sent = pl.multiple_of(base + (1 - side) * share, share)
        mine[node] = acc[:, pl.ds(kept, share), :]
        away[node] = acc[:, pl.ds(sent, share), :]


def top_kernel(width, hops, final, scale, share, *refs):
    place, *refs = refs
    arrived = []
    for pieces in hops:
        arrived.append(refs[:pieces])
        refs = refs[pieces:]
    guess, slope, states = refs[:3]
    refs = refs[3:]
    if final:
        before, _, adjoint, mine, away, acc, zs = refs
    else:
        before = None
        adjoint, acc, zs = refs
    pixels = guess.shape[0]

    @pl.when(place[0] == len(hops))
    def _():
        adjoint[...] = guess[...]

    for hop, pieces in enumerate(arrived):

        @pl.when(place[0] == len(hops) - 1 - hop)
        def _(pieces=pieces):
            row = 0
            for piece in pieces:
                adjoint[pl.ds(row, piece.shape[0]), :] = piece[...]
                row += piece.shape[0]

    blank(zs, 0, width)
    blank(zs, pixels + width, width)
    fill(zs, width, slope[...].astype(f32) * adjoint[...], width)
    grads_into(acc, zs, states, width, scale, before)
    if final:
        hand_out(acc, place[1], mine, away, share)


def top_of(place, arrived, guess, slopes, states, before, after, image, width, scale, share):
    layers, _, pixels, channels = slopes.shape
    final = before is not None
    grad = (9, channels, channels)
    split = (channels // share // 2, 9, share, channels)
    tile = window((pixels, channels), (layers - 1, image), 0)
    pieces = [p for hop in arrived for p in hop]
    in_specs = [pl.BlockSpec(memory_space=pltpu.SMEM)]
    in_specs += [whole(p.shape) for p in pieces] + [whole(guess.shape), tile, tile]
    out_shape = [jax.ShapeDtypeStruct((pixels, channels), f32)]
    scratch = [pltpu.VMEM((3, pixels + 2 * width, channels), bf16)]
    if final:
        in_specs += [whole(grad), pl.BlockSpec(memory_space=pl.ANY)]
        out_shape += [jax.ShapeDtypeStruct(split, f32)] * 2
        scratch.insert(0, pltpu.VMEM(grad, f32))
    else:
        out_shape.append(jax.ShapeDtypeStruct(grad, f32))
    return pl.pallas_call(
        functools.partial(top_kernel, width, [len(hop) for hop in arrived], final, scale, share),
        out_shape=out_shape,
        grid=(1,),
        in_specs=in_specs,
        out_specs=[whole(s.shape) for s in out_shape],
        scratch_shapes=scratch,
        cost_estimate=cost(pixels, channels, 9, pixels * channels * 20),
        compiler_params=limits(36),
        name="top",
    )(place, *pieces, guess, slopes, states, *((before, after) if final else ()))


def inner_kernel(width, final, scale, share, *refs):
    place, adjoint, slope_above, slope, states, kernel = refs[:6]
    refs = list(refs[6:])
    before = refs.pop(0) if final else None
    if final:
        below, mine, away, acc, zs, zs2 = refs
    else:
        below, acc, zs, zs2 = refs
    pixels = adjoint.shape[0]
    for z in (zs, zs2):
        blank(z, 0, width)
        blank(z, pixels + width, width)
    fill(zs, width, slope_above[...].astype(f32) * adjoint[...], width)
    conv_into(
        below, zs, kernel, width,
        lambda s, n, moved: adjoint[pl.ds(s, n), :] + step_size * moved,
    )
    fill(zs2, width, slope[...].astype(f32) * below[...], width)
    grads_into(acc, zs2, states, width, scale, before)
    if final:
        hand_out(acc, place[1], mine, away, share)


def inner_of(place, adjoint, slopes, states, kernels, before, layer, image, width, scale, share):
    pixels, channels = adjoint.shape
    final = before is not None
    grad = (9, channels, channels)
    split = (channels // share // 2, 9, share, channels)
    in_specs = [
        pl.BlockSpec(memory_space=pltpu.SMEM),
        whole((pixels, channels)),
        window((pixels, channels), (layer + 1, image), 0),
        window((pixels, channels), (layer, image), 0),
        window((pixels, channels), (layer, image), 0),
        pl.BlockSpec((None, *kernels.shape[1:]), lambda *_: (layer + 1, 0, 0, 0)),
    ]
    out_shape = [jax.ShapeDtypeStruct((pixels, channels), f32)]
    scratch = [pltpu.VMEM((3, pixels + 2 * width, channels), bf16)] * 2
    if final:
        in_specs.append(whole(grad))
        out_shape += [jax.ShapeDtypeStruct(split, f32)] * 2
        scratch.insert(0, pltpu.VMEM(grad, f32))
    else:
        out_shape.append(jax.ShapeDtypeStruct(grad, f32))
    return pl.pallas_call(
        functools.partial(inner_kernel, width, final, scale, share),
        out_shape=out_shape,
        grid=(1,),
        in_specs=in_specs,
        out_specs=[whole(s.shape) for s in out_shape],
        scratch_shapes=scratch,
        cost_estimate=cost(pixels, channels, 18, pixels * channels * 20),
        compiler_params=limits(36),
        name="inner",
    )(place, adjoint, slopes, slopes, states, kernels, *((before,) if final else ()))


def lower_kernel(width, adjoint, slope, kernel, *refs):
    out, zs = refs[-2:]
    pixels = adjoint.shape[0]
    blank(zs, 0, width)
    blank(zs, pixels + width, width)
    fill(zs, width, slope[...].astype(f32) * adjoint[...], width)
    conv_into(
        out, zs, kernel, width,
        lambda s, n, moved: adjoint[pl.ds(s, n), :] + step_size * moved,
    )


def lower_of(adjoint, slope, kernel, image, images, into, width):
    pixels, channels = adjoint.shape
    return pl.pallas_call(
        functools.partial(lower_kernel, width),
        out_shape=jax.ShapeDtypeStruct((images, pixels, channels), f32),
        grid=(1,),
        in_specs=[
            whole((pixels, channels)),
            whole((pixels, channels)),
            whole(kernel.shape),
        ]
        + [pl.BlockSpec(memory_space=pl.ANY)] * len(into),
        out_specs=pl.BlockSpec((None, pixels, channels), lambda *_: (image, 0, 0)),
        scratch_shapes=[pltpu.VMEM((3, pixels + 2 * width, channels), bf16)],
        input_output_aliases={3: 0} if into else {},
        cost_estimate=cost(pixels, channels, 9, pixels * channels * 12),
        compiler_params=limits(16),
        name="lower",
    )(adjoint, slope, kernel, *into)


def cuts_of(height, hops):
    piece = height // PIECES
    return [
        [0] + [min(height, piece * (k + 1) + hops - 1 - hop) for k in range(PIECES - 1)] + [height]
        for hop in range(hops)
    ]


def chain(place, ends, cuts, guess, slope, kernel, factor, width):
    sections = lax.axis_size("layer")
    images = len(ends)
    height = guess[0].shape[0] // width
    hops = sections - 1
    payload = ends
    arrivals = [[] for _ in range(images)]
    for hop in range(hops):
        pairs = [(sections - 1 - hop, sections - 2 - hop)]
        following = []
        for i in range(images):
            sent, got, tail = [], [], None
            for k, rows in enumerate(payload[i]):
                arrived = lax.ppermute(rows, "layer", pairs)
                got.append(arrived)
                if hop + 1 < hops:
                    low, high = cuts[hop][k : k + 2]
                    first, last = cuts[hop + 1][k : k + 2]
                    passed, tail = stage(
                        place, sections - 2 - hop, arrived, tail, guess[i], slope[i], kernel,
                        list(zip(cuts[0], ends[i])), factor,
                        (first, low, last, high, height), width,
                    )
                    sent.append(passed)
            following.append(sent)
            arrivals[i].append(got)
        payload = following
    return arrivals


def both_sides(pairs):
    return [(2 * a + side, 2 * b + side) for a, b in pairs for side in range(2)]


def join_kernel(place, mine, got, held, *outs):
    held[...] = mine[...] + got[...]
    last = held.shape[0] - 1
    for item, out in enumerate(outs):
        out[...] = held[jnp.where(place[2] == 0, last - item, item)]


def join(place, mine, got):
    nodes, *block = mine.shape
    shapes = [mine.shape] + [tuple(block)] * (nodes - 1)
    return pl.pallas_call(
        join_kernel,
        out_shape=[jax.ShapeDtypeStruct(x, f32) for x in shapes],
        grid=(1,),
        in_specs=[pl.BlockSpec(memory_space=pltpu.SMEM)] + [whole(mine.shape)] * 2,
        out_specs=[whole(x) for x in shapes],
        cost_estimate=pl.CostEstimate(flops=mine.size, bytes_accessed=16 * mine.size, transcendentals=0),
        compiler_params=limits(16),
        name="join",
    )(place, mine, got)


def relay_kernel(place, held, arrived, out):
    out[...] = held[...] + arrived[...]


def relay(place, held, arrived, wave, item):
    last = held.shape[0] - 1
    block = held.shape[1:]

    def which(_, place):
        return (jnp.where(place[2] == wave - 1, last - item, item), 0, 0, 0)

    return pl.pallas_call(
        relay_kernel,
        out_shape=jax.ShapeDtypeStruct(block, f32),
        grid_spec=pltpu.PrefetchScalarGridSpec(
            num_scalar_prefetch=1,
            grid=(1,),
            in_specs=[pl.BlockSpec((None, *block), which), whole(block)],
            out_specs=whole(block),
        ),
        cost_estimate=pl.CostEstimate(
            flops=arrived.size, bytes_accessed=12 * arrived.size, transcendentals=0
        ),
        compiler_params=limits(12),
        name="relay",
    )(place, held, arrived)


def total_kernel(nodes, place, held, *refs):
    arrived, out = refs[: nodes - 1], refs[-1]
    out[...] = held[...]
    for wave, piece in enumerate(arrived, 1):

        @pl.when((place[2] == wave) | (place[2] == nodes - 1 - wave))
        def _(piece=piece):
            out[...] = out[...] + piece[...]


def total(place, held, arrived, layer, layers, into):
    nodes, *block = held.shape
    return pl.pallas_call(
        functools.partial(total_kernel, nodes),
        out_shape=jax.ShapeDtypeStruct((layers, *block), f32),
        grid_spec=pltpu.PrefetchScalarGridSpec(
            num_scalar_prefetch=1,
            grid=(1,),
            in_specs=[pl.BlockSpec((None, *block), lambda _, place: (place[2], 0, 0, 0))]
            + [whole(tuple(block))] * len(arrived)
            + [pl.BlockSpec(memory_space=pl.ANY)] * len(into),
            out_specs=pl.BlockSpec((None, *block), lambda *_: (layer, 0, 0, 0)),
        ),
        input_output_aliases={2 + len(arrived): 0} if into else {},
        cost_estimate=pl.CostEstimate(
            flops=held.size, bytes_accessed=4 * held.size, transcendentals=0
        ),
        compiler_params=limits(12),
        name="total",
    )(place, held, *arrived, *into)


def line_sum(place, mine, away, layer, layers, into):
    replicas = lax.axis_size("dp")
    nodes = replicas // 2
    got = lax.ppermute(away, "dp", [(i, i ^ 1) for i in range(replicas)])
    held, *sends = join(place, mine, got)
    arrived = {}
    for wave in range(1, nodes):
        pairs = both_sides([(wave - 1, wave), (nodes - wave, nodes - 1 - wave)])
        for item in range(nodes - wave):
            out = sends[item]
            if wave > 1:
                out = relay(place, held, arrived[wave - 1, item], wave, item)
            arrived[wave, item] = lax.ppermute(out, "dp", pairs)
    last = [arrived[wave, nodes - 1 - wave] for wave in range(1, nodes)]
    return total(place, held, last, layer, layers, into)


def plain_sum(mine, away):
    nodes, taps, share, channels = mine.shape
    side = lax.axis_index("dp") % 2
    first, second = jnp.where(side == 0, mine, away), jnp.where(side == 0, away, mine)
    terms = jnp.stack([first, second], axis=1).reshape(2 * nodes, taps, share, channels)
    return lax.psum_scatter(terms, "dp", scatter_dimension=0, tiled=False)


def on_device(states, slopes, kernels, guess):
    layers, images, height, width, channels = states.shape
    flat = (layers, images, height * width, channels)
    states, slopes, guess = (x.reshape(flat) for x in (states, slopes, guess))
    replicas = lax.axis_size("dp")
    sections = lax.axis_size("layer")
    share = channels // replicas
    device = lax.axis_index("dp")
    place = jnp.stack([lax.axis_index("layer"), device % 2, device // 2]).astype(jnp.int32)
    cuts = cuts_of(height, sections - 1)
    first = section_end_of(guess, slopes, kernels, 0, cuts[0][:2], width, False)
    *rest, last, slope, kernel = section_end_of(guess, slopes, kernels, 0, cuts[0][1:], width, True)
    ends, lasts, slopes_of = [[*first, *rest]], [last], [slope]
    for i in range(1, images):
        *rest, last, slope = section_end_of(guess, slopes, kernel, i, cuts[0], width, True)
        ends.append(rest)
        lasts.append(last)
        slopes_of.append(slope)
    arrivals = chain(place, ends, cuts, lasts, slopes_of, kernel, step_size * layers, width)
    scale = step_size / (images * replicas)
    adjoints = [None] * images
    grads = [None] * layers
    for i in range(images):
        final = i == images - 1
        for layer in range(layers - 1, -1, -1):
            if layer == layers - 1:
                adjoints[i], *grads[layer] = top_of(
                    place, arrivals[i], lasts[i], slopes, states,
                    grads[layer][0] if final else None, adjoints[i - 1] if final else None, i,
                    width, scale if final else 1.0, share,
                )
            else:
                adjoints[i], *grads[layer] = inner_of(
                    place, adjoints[i], slopes, states, kernels,
                    grads[layer][0] if final else None, layer, i, width,
                    scale if final else 1.0, share,
                )
    lower = ()
    for i in range(images):
        lower = (lower_of(adjoints[i], slopes_of[i], kernel, i, images, lower, width),)
    if replicas in (4, 8):
        gradients = ()
        for layer in range(layers - 1, -1, -1):
            gradients = (line_sum(place, *grads[layer], layer, layers, gradients),)
        gradients = gradients[0]
    else:
        gradients = jnp.stack([plain_sum(*grads[layer]) for layer in range(layers)])
    return lower[0].reshape(1, images, height, width, channels), gradients


def solution(mesh):
    return jax.shard_map(
        on_device,
        mesh=mesh,
        in_specs=(
            P("layer", "dp", None, None, None),
            P("layer", "dp", None, None, None),
            P("layer", None, None, None),
            P("layer", "dp", None, None, None),
        ),
        out_specs=(P("layer", "dp", None, None, None), P("layer", None, "dp", None)),
        check_vma=False,
    )
```

```python
import functools

import jax
import jax.numpy as jnp
from jax import lax
from jax.experimental import pallas as pl
from jax.experimental.pallas import tpu as pltpu
from jax.sharding import PartitionSpec as P


PIECES = 4

step_size = 0.5

f32 = jnp.float32
bf16 = jnp.bfloat16


def tile_of(size):
    if size <= 384:
        return size
    for tile in (256, 128, 64, 32):
        if size % tile == 0:
            return tile
    return size


def limits(megabytes):
    return pltpu.CompilerParams(vmem_limit_bytes=megabytes << 20)


def fill(zs, first, z, width):
    count = z.shape[0]
    column = lax.broadcasted_iota(jnp.int32, z.shape, 0) % width
    after = jnp.where(column == width - 1, 0.0, pltpu.roll(z, count - 1, 0))
    before = jnp.where(column == 0, 0.0, pltpu.roll(z, 1, 0))
    rows = pl.ds(first, count)
    zs[0, rows, :] = after.astype(bf16)
    zs[1, rows, :] = z.astype(bf16)
    zs[2, rows, :] = before.astype(bf16)


def blank(zs, first, count):
    zs[:, pl.ds(first, count), :] = jnp.zeros((3, count, zs.shape[2]), bf16)


def taps_at(zs, kernel_ref, start, size, width):
    total = None
    for a in range(3):
        for b in range(3):
            rows = zs[b, pl.ds(start + (2 - a) * width, size), :]
            term = lax.dot_general(
                rows, kernel_ref[3 * a + b], (((1,), (1,)), ((), ())), preferred_element_type=f32
            )
            total = term if total is None else total + term
    return total


def conv_into(out, zs, kernel_ref, width, finish):
    for start, tile in tiles_of(out.shape[0]):
        out[pl.ds(start, tile), :] = finish(start, tile, taps_at(zs, kernel_ref, start, tile, width))


def window(shape, lead, first):
    spec = (None,) * len(lead) + (pl.Element(shape[0]), pl.Element(shape[1]))
    return pl.BlockSpec(spec, lambda *_: (*lead, first, 0))


def cost(rows, channels, taps, moved):
    return pl.CostEstimate(
        flops=2 * rows * channels * channels * taps, bytes_accessed=moved, transcendentals=0
    )


def whole(shape):
    return pl.BlockSpec(shape, lambda *_: (0,) * len(shape))


def end_kernel(width, first_row, low_row, counts, extra, copies, *refs):
    guess, slope, kernel = refs[:3]
    outs, zs = refs[3 + extra : -1], refs[-1]
    lead = (first_row - (low_row - 1)) * width
    count = guess.shape[0]
    if lead:
        blank(zs, 0, lead)
    fill(zs, lead, slope[...].astype(f32) * guess[...], width)
    rest = zs.shape[1] - lead - count
    if rest:
        blank(zs, lead + count, rest)
    base = 0
    inside = (low_row - first_row) * width
    for out in outs[: len(counts)]:
        for start, size in tiles_of(out.shape[0]):
            moved = taps_at(zs, kernel, base + start, size, width)
            rows = pl.ds(inside + base + start, size)
            out[pl.ds(start, size), :] = guess[rows, :] + step_size * moved
        base += out.shape[0]
    for source, out in zip(copies, outs[len(counts) :]):
        out[...] = refs[source][...]


def tiles_of(count):
    tile = tile_of(count)
    return [(start, tile) for start in range(0, count, tile)]


def in_hbm(x):
    return pltpu.with_memory_space_constraint(x, pltpu.HBM)


def section_end_of(guess, slopes, kernel, image, cuts, width, keep, after=()):
    layers, _, pixels, channels = guess.shape
    height = pixels // width
    low, high = cuts[0], cuts[-1]
    first, last = max(low - 1, 0), min(high + 1, height)
    rows = window(((last - first) * width, channels), (0, image), first * width)
    shapes = [((b - a) * width, channels) for a, b in zip(cuts, cuts[1:])]
    taps = kernel.shape[-3:]
    kernel_spec = whole(taps)
    if kernel.ndim == 4:
        kernel, kernel_spec = in_hbm(kernel), pl.BlockSpec((None, *taps), lambda *_: (0, 0, 0, 0))
    args, in_specs = [in_hbm(guess), in_hbm(slopes), kernel], [rows, rows, kernel_spec]
    out_shape = [jax.ShapeDtypeStruct(x, f32) for x in shapes]
    copies = []
    if keep:
        args += [in_hbm(guess), in_hbm(slopes)]
        in_specs += [window((pixels, channels), (layers - 1, image), 0)]
        in_specs += [window((pixels, channels), (0, image), 0)]
        out_shape += [jax.ShapeDtypeStruct((pixels, channels), t) for t in (f32, slopes.dtype)]
        copies = [3, 4]
        if kernel.ndim == 4:
            out_shape.append(jax.ShapeDtypeStruct(taps, kernel.dtype))
            copies.append(2)
    args += after
    in_specs += [pl.BlockSpec(memory_space=pltpu.SMEM)] * len(after)
    return pl.pallas_call(
        functools.partial(end_kernel, width, first, low, shapes, len(args) - 3, copies),
        out_shape=out_shape,
        grid=(1,),
        in_specs=in_specs,
        out_specs=[whole(x.shape) for x in out_shape],
        scratch_shapes=[pltpu.VMEM((3, (high - low + 2) * width, channels), bf16)],
        cost_estimate=cost((high - low) * width, channels, 9, (high - low) * width * channels * 12),
        compiler_params=limits(24),
        name="section_end",
    )(*args)


def stage_kernel(width, factor, first_row, low_row, has_tail, gives_tail, spans, owner, *refs):
    place, *refs = refs
    tail = refs.pop(0) if has_tail else None
    arrived, guess, slope, kernel = refs[:4]
    ends = refs[4 : 4 + len(spans)]
    out = refs[4 + len(spans)]
    tail_out = refs[5 + len(spans)] if gives_tail else None
    field, zs = refs[-2:]
    above = max(first_row - 1, 0)
    kept = (low_row - above) * width
    new = arrived.shape[0]

    @pl.when(place[0] == owner)
    def _():
        if has_tail:
            field[pl.ds(0, kept), :] = tail[...]
        field[pl.ds(kept, new), :] = arrived[...] - guess[...]
        lead = (above - (first_row - 1)) * width
        count = kept + new
        if lead:
            blank(zs, 0, lead)
        fill(zs, lead, slope[...].astype(f32) * field[...], width)
        rest = zs.shape[1] - lead - count
        if rest:
            blank(zs, lead + count, rest)
        if gives_tail:
            tail_out[...] = field[pl.ds(count - 2 * width, 2 * width), :]
        base = (first_row - above) * width
        for start, size in tiles_of(out.shape[0]):
            moved = taps_at(zs, kernel, start, size, width)
            out[pl.ds(start, size), :] = field[pl.ds(base + start, size), :] + factor * moved
        for (top, begin, size), end in zip(spans, ends):
            rows = pl.ds(top, size)
            out[rows, :] = out[rows, :] + end[pl.ds(begin, size), :]


def stage(place, owner, arrived, tail, guess, slope, kernel, ends, factor, rows, width):
    first, low, last, high, height = rows
    channels = guess.shape[1]
    above = max(first - 1, 0)
    gives_tail = high < height
    count = (last - first) * width
    used, spans = [], []
    for begin, piece in ends:
        stop = begin + piece.shape[0] // width
        a, b = max(begin, first), min(stop, last)
        if a < b:
            used.append(piece)
            spans.append(((a - first) * width, (a - begin) * width, (b - a) * width))
    in_specs = [pl.BlockSpec(memory_space=pltpu.SMEM)]
    in_specs += [] if tail is None else [whole(tail.shape)]
    in_specs += [
        whole(arrived.shape),
        window(arrived.shape, (), low * width),
        window(((high - above) * width, channels), (), above * width),
        whole(kernel.shape),
    ] + [whole(piece.shape) for piece in used]
    out_shape = [jax.ShapeDtypeStruct((count, channels), f32)]
    if gives_tail:
        out_shape.append(jax.ShapeDtypeStruct((2 * width, channels), f32))
    results = pl.pallas_call(
        functools.partial(
            stage_kernel, width, factor, first, low, tail is not None, gives_tail,
            spans, owner,
        ),
        out_shape=out_shape,
        grid=(1,),
        in_specs=in_specs,
        out_specs=[whole(s.shape) for s in out_shape],
        scratch_shapes=[
            pltpu.VMEM(((high - above) * width, channels), f32),
            pltpu.VMEM((3, count + 2 * width, channels), bf16),
        ],
        cost_estimate=cost(count, channels, 9, count * channels * 20),
        compiler_params=limits(12),
        name="stage",
    )(place, *(() if tail is None else (tail,)), arrived, guess, slope, kernel, *used)
    return results[0], (results[1] if gives_tail else None)


def grads_into(acc, zs, states, width, scale, before):
    pixels = states.shape[0]
    turned = states[...].T
    for a in range(3):
        for b in range(3):
            rows = zs[b, pl.ds((2 - a) * width, pixels), :]
            term = lax.dot_general(
                turned, rows, (((1,), (0,)), ((), ())), preferred_element_type=f32
            )
            if before is not None:
                term = term + before[3 * a + b]
            acc[3 * a + b] = term * scale if scale != 1.0 else term


def hand_out(acc, side, outs, share):
    nodes = len(outs)
    for group in range(nodes // 2):
        for place, node in enumerate((group, nodes - 1 - group)):
            base = 2 * node * share
            kept = pl.multiple_of(base + side * share, share)
            sent = pl.multiple_of(base + (1 - side) * share, share)
            outs[2 * group][place] = acc[:, pl.ds(kept, share), :]
            outs[2 * group + 1][place] = acc[:, pl.ds(sent, share), :]


def top_kernel(width, hops, final, scale, share, *refs):
    place, *refs = refs
    arrived = []
    for pieces in hops:
        arrived.append(refs[:pieces])
        refs = refs[pieces:]
    guess, slope, states = refs[:3]
    refs = refs[3:]
    if final:
        before, _, adjoint, *outs, acc, zs = refs
    else:
        before = None
        adjoint, acc, zs = refs
    pixels = guess.shape[0]

    @pl.when(place[0] == len(hops))
    def _():
        adjoint[...] = guess[...]

    for hop, pieces in enumerate(arrived):

        @pl.when(place[0] == len(hops) - 1 - hop)
        def _(pieces=pieces):
            row = 0
            for piece in pieces:
                adjoint[pl.ds(row, piece.shape[0]), :] = piece[...]
                row += piece.shape[0]

    blank(zs, 0, width)
    blank(zs, pixels + width, width)
    fill(zs, width, slope[...].astype(f32) * adjoint[...], width)
    grads_into(acc, zs, states, width, scale, before)
    if final:
        hand_out(acc, place[1], outs, share)


def top_of(place, arrived, guess, slopes, states, before, after, image, width, scale, share):
    layers, _, pixels, channels = slopes.shape
    final = before is not None
    grad = (9, channels, channels)
    split = (2, 9, share, channels)
    tile = window((pixels, channels), (layers - 1, image), 0)
    pieces = [p for hop in arrived for p in hop]
    in_specs = [pl.BlockSpec(memory_space=pltpu.SMEM)]
    in_specs += [whole(p.shape) for p in pieces] + [whole(guess.shape), tile, tile]
    out_shape = [jax.ShapeDtypeStruct((pixels, channels), f32)]
    scratch = [pltpu.VMEM((3, pixels + 2 * width, channels), bf16)]
    if final:
        in_specs += [whole(grad), pl.BlockSpec(memory_space=pltpu.HBM)]
        out_shape += [jax.ShapeDtypeStruct(split, f32)] * (channels // share // 2)
        scratch.insert(0, pltpu.VMEM(grad, f32))
    else:
        out_shape.append(jax.ShapeDtypeStruct(grad, f32))
    return pl.pallas_call(
        functools.partial(top_kernel, width, [len(hop) for hop in arrived], final, scale, share),
        out_shape=out_shape,
        grid=(1,),
        in_specs=in_specs,
        out_specs=[whole(s.shape) for s in out_shape],
        scratch_shapes=scratch,
        cost_estimate=cost(pixels, channels, 9, pixels * channels * 20),
        compiler_params=limits(24),
        name="top",
    )(place, *pieces, guess, slopes, states, *((before, in_hbm(after)) if final else ()))


def inner_kernel(width, final, scale, share, *refs):
    place, adjoint, slope_above, slope, states, kernel = refs[:6]
    refs = list(refs[6:])
    before = refs.pop(0) if final else None
    if final:
        below, *outs, acc, zs, zs2 = refs
    else:
        below, acc, zs, zs2 = refs
    pixels = adjoint.shape[0]
    for z in (zs, zs2):
        blank(z, 0, width)
        blank(z, pixels + width, width)
    fill(zs, width, slope_above[...].astype(f32) * adjoint[...], width)
    conv_into(
        below, zs, kernel, width,
        lambda s, n, moved: adjoint[pl.ds(s, n), :] + step_size * moved,
    )
    fill(zs2, width, slope[...].astype(f32) * below[...], width)
    grads_into(acc, zs2, states, width, scale, before)
    if final:
        hand_out(acc, place[1], outs, share)


def inner_of(place, adjoint, slopes, states, kernels, before, layer, image, width, scale, share):
    pixels, channels = adjoint.shape
    final = before is not None
    grad = (9, channels, channels)
    split = (2, 9, share, channels)
    in_specs = [
        pl.BlockSpec(memory_space=pltpu.SMEM),
        whole((pixels, channels)),
        window((pixels, channels), (layer + 1, image), 0),
        window((pixels, channels), (layer, image), 0),
        window((pixels, channels), (layer, image), 0),
        pl.BlockSpec((None, *kernels.shape[1:]), lambda *_: (layer + 1, 0, 0, 0)),
    ]
    out_shape = [jax.ShapeDtypeStruct((pixels, channels), f32)]
    scratch = [pltpu.VMEM((3, pixels + 2 * width, channels), bf16)] * 2
    if final:
        in_specs.append(whole(grad))
        out_shape += [jax.ShapeDtypeStruct(split, f32)] * (channels // share // 2)
        scratch.insert(0, pltpu.VMEM(grad, f32))
    else:
        out_shape.append(jax.ShapeDtypeStruct(grad, f32))
    return pl.pallas_call(
        functools.partial(inner_kernel, width, final, scale, share),
        out_shape=out_shape,
        grid=(1,),
        in_specs=in_specs,
        out_specs=[whole(s.shape) for s in out_shape],
        scratch_shapes=scratch,
        cost_estimate=cost(pixels, channels, 18, pixels * channels * 20),
        compiler_params=limits(24),
        name="inner",
    )(place, adjoint, slopes, slopes, states, kernels, *((before,) if final else ()))


def lower_kernel(width, adjoint, slope, kernel, *refs):
    out, zs = refs[-2:]
    pixels = adjoint.shape[0]
    blank(zs, 0, width)
    blank(zs, pixels + width, width)
    fill(zs, width, slope[...].astype(f32) * adjoint[...], width)
    conv_into(
        out, zs, kernel, width,
        lambda s, n, moved: adjoint[pl.ds(s, n), :] + step_size * moved,
    )


def lower_of(adjoint, slope, kernel, image, images, into, width):
    pixels, channels = adjoint.shape
    return pl.pallas_call(
        functools.partial(lower_kernel, width),
        out_shape=jax.ShapeDtypeStruct((images, pixels, channels), f32),
        grid=(1,),
        in_specs=[
            whole((pixels, channels)),
            whole((pixels, channels)),
            whole(kernel.shape),
        ]
        + [pl.BlockSpec(memory_space=pl.ANY)] * len(into),
        out_specs=pl.BlockSpec((None, pixels, channels), lambda *_: (image, 0, 0)),
        scratch_shapes=[pltpu.VMEM((3, pixels + 2 * width, channels), bf16)],
        input_output_aliases={3: 0} if into else {},
        cost_estimate=cost(pixels, channels, 9, pixels * channels * 12),
        compiler_params=limits(16),
        name="lower",
    )(adjoint, slope, kernel, *into)


def cuts_of(height, hops):
    piece = height // PIECES
    return [
        [0] + [min(height, piece * (k + 1) + hops - 1 - hop) for k in range(PIECES - 1)] + [height]
        for hop in range(hops)
    ]


def chain(place, ends, cuts, guess, slope, kernel, factor, width):
    sections = lax.axis_size("layer")
    images = len(ends)
    height = guess[0].shape[0] // width
    hops = sections - 1
    payload = ends
    arrivals = [[] for _ in range(images)]
    for hop in range(hops):
        pairs = [(sections - 1 - hop, sections - 2 - hop)]
        following = []
        for i in range(images):
            sent, got, tail = [], [], None
            for k, rows in enumerate(payload[i]):
                arrived = lax.ppermute(rows, "layer", pairs)
                got.append(arrived)
                if hop + 1 < hops:
                    low, high = cuts[hop][k : k + 2]
                    first, last = cuts[hop + 1][k : k + 2]
                    passed, tail = stage(
                        place, sections - 2 - hop, arrived, tail, guess[i], slope[i], kernel,
                        list(zip(cuts[0], ends[i])), factor,
                        (first, low, last, high, height), width,
                    )
                    sent.append(passed)
            following.append(sent)
            arrivals[i].append(got)
        payload = following
    return arrivals


def both_sides(pairs):
    return [(2 * a + side, 2 * b + side) for a, b in pairs for side in range(2)]


def join_kernel(items, nodes, place, mine, got, held, *outs):
    held[...] = mine[...] + got[...]
    for item, out in zip(items, outs):
        out[...] = held[which_of(item, nodes, place[2] == 0)]


def which_of(item, nodes, upward):
    high = jnp.where(upward, 1, 0)
    return high if 2 * item < nodes else 1 - high


def join(place, mine, got, items, nodes):
    block = mine.shape[1:]
    shapes = [mine.shape] + [block] * len(items)
    return pl.pallas_call(
        functools.partial(join_kernel, items, nodes),
        out_shape=[jax.ShapeDtypeStruct(x, f32) for x in shapes],
        grid=(1,),
        in_specs=[pl.BlockSpec(memory_space=pltpu.SMEM)] + [whole(mine.shape)] * 2,
        out_specs=[whole(x) for x in shapes],
        cost_estimate=pl.CostEstimate(
            flops=mine.size, bytes_accessed=16 * mine.size, transcendentals=0
        ),
        compiler_params=limits(16),
        name="join",
    )(place, mine, got)


def relay_kernel(place, held, arrived, out):
    out[...] = held[...] + arrived[...]


def relay(place, held, arrived, wave, item, nodes):
    block = arrived.shape

    def which(_, place):
        return (which_of(item, nodes, place[2] == wave - 1), 0, 0, 0)

    return pl.pallas_call(
        relay_kernel,
        out_shape=jax.ShapeDtypeStruct(block, f32),
        grid_spec=pltpu.PrefetchScalarGridSpec(
            num_scalar_prefetch=1,
            grid=(1,),
            in_specs=[pl.BlockSpec((None, *block), which), whole(block)],
            out_specs=whole(block),
        ),
        cost_estimate=pl.CostEstimate(
            flops=arrived.size, bytes_accessed=12 * arrived.size, transcendentals=0
        ),
        compiler_params=limits(12),
        name="relay",
    )(place, held, arrived)


def total_kernel(nodes, place, *refs):
    held, arrived, out = refs[: nodes // 2], refs[nodes // 2 : nodes // 2 + nodes - 1], refs[-1]
    node = place[2]
    for group, block in enumerate(held):

        @pl.when((node == group) | (node == nodes - 1 - group))
        def _(block=block):
            out[...] = block[...]

    for wave, piece in enumerate(arrived, 1):

        @pl.when((node == wave) | (node == nodes - 1 - wave))
        def _(piece=piece):
            out[...] = out[...] + piece[...]


def total(place, held, arrived, layer, layers, into):
    nodes = 2 * len(held)
    block = held[0].shape[1:]

    def which(_, place):
        return (jnp.where(2 * place[2] < nodes, 0, 1), 0, 0, 0)

    return pl.pallas_call(
        functools.partial(total_kernel, nodes),
        out_shape=jax.ShapeDtypeStruct((layers, *block), f32),
        grid_spec=pltpu.PrefetchScalarGridSpec(
            num_scalar_prefetch=1,
            grid=(1,),
            in_specs=[pl.BlockSpec((None, *block), which)] * len(held)
            + [whole(block)] * len(arrived)
            + [pl.BlockSpec(memory_space=pl.ANY)] * len(into),
            out_specs=pl.BlockSpec((None, *block), lambda *_: (layer, 0, 0, 0)),
        ),
        input_output_aliases={1 + len(held) + len(arrived): 0} if into else {},
        cost_estimate=pl.CostEstimate(
            flops=nodes * arrived[0].size, bytes_accessed=12 * arrived[0].size, transcendentals=0
        ),
        compiler_params=limits(12),
        name="total",
    )(place, *held, *arrived, *into)


def line_sum(place, terms, layer, layers, into):
    replicas = lax.axis_size("dp")
    nodes = replicas // 2
    got = []
    for group in range(nodes // 2):
        pairs = [(i, i ^ 1) for i in range(replicas)]
        got.append(lax.ppermute(terms[2 * group + 1], "dp", pairs))
    held, sends = [], {}
    for group in range(nodes // 2):
        items = [item for item in (group, nodes - 1 - group) if item < nodes - 1]
        both, *outs = join(place, terms[2 * group], got[group], items, nodes)
        held.append(both)
        sends.update(zip(items, outs))
    arrived = {}
    for wave in range(1, nodes):
        pairs = both_sides([(wave - 1, wave), (nodes - wave, nodes - 1 - wave)])
        for item in range(nodes - wave):
            out = sends[item]
            if wave > 1:
                group = held[min(item, nodes - 1 - item)]
                out = relay(place, group, arrived[wave - 1, item], wave, item, nodes)
            arrived[wave, item] = lax.ppermute(out, "dp", pairs)
    last = [arrived[wave, nodes - 1 - wave] for wave in range(1, nodes)]
    return total(place, held, last, layer, layers, into)


def plain_sum(terms):
    nodes = len(terms)
    taps, share, channels = terms[0].shape[1:]
    side = lax.axis_index("dp") % 2
    order = [(min(k, nodes - 1 - k), int(2 * k >= nodes)) for k in range(nodes)]
    mine = jnp.stack([terms[2 * group][place] for group, place in order])
    away = jnp.stack([terms[2 * group + 1][place] for group, place in order])
    first, second = jnp.where(side == 0, mine, away), jnp.where(side == 0, away, mine)
    terms = jnp.stack([first, second], axis=1).reshape(2 * nodes, taps, share, channels)
    return lax.psum_scatter(terms, "dp", scatter_dimension=0, tiled=False)


def on_device(states, slopes, kernels, guess):
    layers, images, height, width, channels = states.shape
    flat = (layers, images, height * width, channels)
    states, slopes, guess = (x.reshape(flat) for x in (states, slopes, guess))
    replicas = lax.axis_size("dp")
    sections = lax.axis_size("layer")
    share = channels // replicas
    device = lax.axis_index("dp")
    place = jnp.stack([lax.axis_index("layer"), device % 2, device // 2]).astype(jnp.int32)
    cuts = cuts_of(height, sections - 1)
    first = section_end_of(guess, slopes, kernels, 0, cuts[0][:2], width, False)
    *rest, last, slope, kernel = section_end_of(
        guess, slopes, kernels, 0, cuts[0][1:], width, True, [place]
    )
    ends, lasts, slopes_of = [[*first, *rest]], [last], [slope]
    for i in range(1, images):
        *rest, last, slope = section_end_of(guess, slopes, kernel, i, cuts[0], width, True)
        ends.append(rest)
        lasts.append(last)
        slopes_of.append(slope)
    arrivals = chain(place, ends, cuts, lasts, slopes_of, kernel, step_size * layers, width)
    scale = step_size / (images * replicas)
    adjoints = [None] * images
    grads = [None] * layers
    lower = ()
    for i in range(images):
        final = i == images - 1
        for layer in range(layers - 1, -1, -1):
            if layer == layers - 1:
                adjoints[i], *grads[layer] = top_of(
                    place, arrivals[i], lasts[i], slopes, states,
                    grads[layer][0] if final else None, lower[0] if final else None, i,
                    width, scale if final else 1.0, share,
                )
            else:
                adjoints[i], *grads[layer] = inner_of(
                    place, adjoints[i], slopes, states, kernels,
                    grads[layer][0] if final else None, layer, i, width,
                    scale if final else 1.0, share,
                )
        lower = (lower_of(adjoints[i], slopes_of[i], kernel, i, images, lower, width),)
    if replicas in (4, 8):
        gradients = ()
        for layer in range(layers - 1, -1, -1):
            gradients = (line_sum(place, grads[layer], layer, layers, gradients),)
        gradients = gradients[0]
    else:
        gradients = jnp.stack([plain_sum(grads[layer]) for layer in range(layers)])
    return lower[0].reshape(1, images, height, width, channels), gradients


def solution(mesh):
    return jax.shard_map(
        on_device,
        mesh=mesh,
        in_specs=(
            P("layer", "dp", None, None, None),
            P("layer", "dp", None, None, None),
            P("layer", None, None, None),
            P("layer", "dp", None, None, None),
        ),
        out_specs=(P("layer", "dp", None, None, None), P("layer", None, "dp", None)),
        check_vma=False,
    )
```

```python
import functools

import jax
import jax.numpy as jnp
from jax import lax
from jax.experimental import pallas as pl
from jax.experimental.pallas import tpu as pltpu
from jax.sharding import PartitionSpec as P


PIECES = 4

step_size = 0.5

f32 = jnp.float32
bf16 = jnp.bfloat16


def tile_of(size):
    if size <= 384:
        return size
    for tile in (256, 128, 64, 32):
        if size % tile == 0:
            return tile
    return size


def limits(megabytes):
    return pltpu.CompilerParams(vmem_limit_bytes=megabytes << 20)


def fill(zs, first, z, width):
    count = z.shape[0]
    column = lax.broadcasted_iota(jnp.int32, z.shape, 0) % width
    after = jnp.where(column == width - 1, 0.0, pltpu.roll(z, count - 1, 0))
    before = jnp.where(column == 0, 0.0, pltpu.roll(z, 1, 0))
    rows = pl.ds(first, count)
    zs[0, rows, :] = after.astype(bf16)
    zs[1, rows, :] = z.astype(bf16)
    zs[2, rows, :] = before.astype(bf16)


def blank(zs, first, count):
    zs[:, pl.ds(first, count), :] = jnp.zeros((3, count, zs.shape[2]), bf16)


def taps_at(zs, kernel_ref, start, size, width):
    total = None
    for a in range(3):
        for b in range(3):
            rows = zs[b, pl.ds(start + (2 - a) * width, size), :]
            term = lax.dot_general(
                rows, kernel_ref[3 * a + b], (((1,), (1,)), ((), ())), preferred_element_type=f32
            )
            total = term if total is None else total + term
    return total


def conv_into(out, zs, kernel_ref, width, finish):
    for start, tile in tiles_of(out.shape[0]):
        out[pl.ds(start, tile), :] = finish(start, tile, taps_at(zs, kernel_ref, start, tile, width))


def window(shape, lead, first):
    spec = (None,) * len(lead) + (pl.Element(shape[0]), pl.Element(shape[1]))
    return pl.BlockSpec(spec, lambda *_: (*lead, first, 0))


def cost(rows, channels, taps, moved):
    return pl.CostEstimate(
        flops=2 * rows * channels * channels * taps, bytes_accessed=moved, transcendentals=0
    )


def whole(shape):
    return pl.BlockSpec(shape, lambda *_: (0,) * len(shape))


def end_kernel(width, first_row, low_row, counts, extra, copies, *refs):
    guess, slope, kernel = refs[:3]
    outs, zs = refs[3 + extra : -1], refs[-1]
    lead = (first_row - (low_row - 1)) * width
    count = guess.shape[0]
    if lead:
        blank(zs, 0, lead)
    fill(zs, lead, slope[...].astype(f32) * guess[...], width)
    rest = zs.shape[1] - lead - count
    if rest:
        blank(zs, lead + count, rest)
    base = 0
    inside = (low_row - first_row) * width
    for out in outs[: len(counts)]:
        for start, size in tiles_of(out.shape[0]):
            moved = taps_at(zs, kernel, base + start, size, width)
            rows = pl.ds(inside + base + start, size)
            out[pl.ds(start, size), :] = guess[rows, :] + step_size * moved
        base += out.shape[0]
    for source, out in zip(copies, outs[len(counts) :]):
        out[...] = refs[source][...]


def tiles_of(count):
    tile = tile_of(count)
    return [(start, tile) for start in range(0, count, tile)]


def in_hbm(x):
    return pltpu.with_memory_space_constraint(x, pltpu.HBM)


def section_end_of(guess, slopes, kernel, image, cuts, width, keep, after=()):
    layers, _, pixels, channels = guess.shape
    height = pixels // width
    low, high = cuts[0], cuts[-1]
    first, last = max(low - 1, 0), min(high + 1, height)
    rows = window(((last - first) * width, channels), (0, image), first * width)
    shapes = [((b - a) * width, channels) for a, b in zip(cuts, cuts[1:])]
    taps = kernel.shape[-3:]
    kernel_spec = whole(taps)
    if kernel.ndim == 4:
        kernel, kernel_spec = in_hbm(kernel), pl.BlockSpec((None, *taps), lambda *_: (0, 0, 0, 0))
    args, in_specs = [in_hbm(guess), in_hbm(slopes), kernel], [rows, rows, kernel_spec]
    out_shape = [jax.ShapeDtypeStruct(x, f32) for x in shapes]
    copies = []
    if keep:
        args += [in_hbm(guess), in_hbm(slopes)]
        in_specs += [window((pixels, channels), (layers - 1, image), 0)]
        in_specs += [window((pixels, channels), (0, image), 0)]
        out_shape += [jax.ShapeDtypeStruct((pixels, channels), t) for t in (f32, slopes.dtype)]
        copies = [3, 4]
        if kernel.ndim == 4:
            out_shape.append(jax.ShapeDtypeStruct(taps, kernel.dtype))
            copies.append(2)
    args += after
    in_specs += [pl.BlockSpec(memory_space=pltpu.SMEM)] * len(after)
    return pl.pallas_call(
        functools.partial(end_kernel, width, first, low, shapes, len(args) - 3, copies),
        out_shape=out_shape,
        grid=(1,),
        in_specs=in_specs,
        out_specs=[whole(x.shape) for x in out_shape],
        scratch_shapes=[pltpu.VMEM((3, (high - low + 2) * width, channels), bf16)],
        cost_estimate=cost((high - low) * width, channels, 9, (high - low) * width * channels * 12),
        compiler_params=limits(24),
        name="section_end",
    )(*args)


def stage_kernel(width, factor, first_row, low_row, has_tail, gives_tail, spans, owner, *refs):
    place, *refs = refs
    tail = refs.pop(0) if has_tail else None
    arrived, guess, slope, kernel = refs[:4]
    ends = refs[4 : 4 + len(spans)]
    out = refs[4 + len(spans)]
    tail_out = refs[5 + len(spans)] if gives_tail else None
    field, zs = refs[-2:]
    above = max(first_row - 1, 0)
    kept = (low_row - above) * width
    new = arrived.shape[0]

    @pl.when(place[0] == owner)
    def _():
        if has_tail:
            field[pl.ds(0, kept), :] = tail[...]
        field[pl.ds(kept, new), :] = arrived[...] - guess[...]
        lead = (above - (first_row - 1)) * width
        count = kept + new
        if lead:
            blank(zs, 0, lead)
        fill(zs, lead, slope[...].astype(f32) * field[...], width)
        rest = zs.shape[1] - lead - count
        if rest:
            blank(zs, lead + count, rest)
        if gives_tail:
            tail_out[...] = field[pl.ds(count - 2 * width, 2 * width), :]
        base = (first_row - above) * width
        for start, size in tiles_of(out.shape[0]):
            moved = taps_at(zs, kernel, start, size, width)
            out[pl.ds(start, size), :] = field[pl.ds(base + start, size), :] + factor * moved
        for (top, begin, size), end in zip(spans, ends):
            rows = pl.ds(top, size)
            out[rows, :] = out[rows, :] + end[pl.ds(begin, size), :]


def stage(place, owner, arrived, tail, guess, slope, kernel, ends, factor, rows, width):
    first, low, last, high, height = rows
    channels = guess.shape[1]
    above = max(first - 1, 0)
    gives_tail = high < height
    count = (last - first) * width
    used, spans = [], []
    for begin, piece in ends:
        stop = begin + piece.shape[0] // width
        a, b = max(begin, first), min(stop, last)
        if a < b:
            used.append(piece)
            spans.append(((a - first) * width, (a - begin) * width, (b - a) * width))
    in_specs = [pl.BlockSpec(memory_space=pltpu.SMEM)]
    in_specs += [] if tail is None else [whole(tail.shape)]
    in_specs += [
        whole(arrived.shape),
        window(arrived.shape, (), low * width),
        window(((high - above) * width, channels), (), above * width),
        whole(kernel.shape),
    ] + [whole(piece.shape) for piece in used]
    out_shape = [jax.ShapeDtypeStruct((count, channels), f32)]
    if gives_tail:
        out_shape.append(jax.ShapeDtypeStruct((2 * width, channels), f32))
    results = pl.pallas_call(
        functools.partial(
            stage_kernel, width, factor, first, low, tail is not None, gives_tail,
            spans, owner,
        ),
        out_shape=out_shape,
        grid=(1,),
        in_specs=in_specs,
        out_specs=[whole(s.shape) for s in out_shape],
        scratch_shapes=[
            pltpu.VMEM(((high - above) * width, channels), f32),
            pltpu.VMEM((3, count + 2 * width, channels), bf16),
        ],
        cost_estimate=cost(count, channels, 9, count * channels * 20),
        compiler_params=limits(12),
        name="stage",
    )(place, *(() if tail is None else (tail,)), arrived, guess, slope, kernel, *used)
    return results[0], (results[1] if gives_tail else None)


def grads_into(acc, zs, states, width, scale, before):
    pixels = states.shape[0]
    turned = states[...].T
    for a in range(3):
        for b in range(3):
            rows = zs[b, pl.ds((2 - a) * width, pixels), :]
            term = lax.dot_general(
                turned, rows, (((1,), (0,)), ((), ())), preferred_element_type=f32
            )
            if before is not None:
                term = term + before[3 * a + b]
            acc[3 * a + b] = term * scale if scale != 1.0 else term


def hand_out(acc, side, outs, share):
    nodes = len(outs)
    for group in range(nodes // 2):
        for place, node in enumerate((group, nodes - 1 - group)):
            base = 2 * node * share
            kept = pl.multiple_of(base + side * share, share)
            sent = pl.multiple_of(base + (1 - side) * share, share)
            outs[2 * group][place] = acc[:, pl.ds(kept, share), :]
            outs[2 * group + 1][place] = acc[:, pl.ds(sent, share), :]


def top_kernel(width, hops, final, scale, share, *refs):
    place, *refs = refs
    arrived = []
    for pieces in hops:
        arrived.append(refs[:pieces])
        refs = refs[pieces:]
    guess, slope, states = refs[:3]
    refs = refs[3:]
    if final:
        before, _, adjoint, *outs, acc, zs = refs
    else:
        before = None
        adjoint, acc, zs = refs
    pixels = guess.shape[0]

    @pl.when(place[0] == len(hops))
    def _():
        adjoint[...] = guess[...]

    for hop, pieces in enumerate(arrived):

        @pl.when(place[0] == len(hops) - 1 - hop)
        def _(pieces=pieces):
            row = 0
            for piece in pieces:
                adjoint[pl.ds(row, piece.shape[0]), :] = piece[...]
                row += piece.shape[0]

    blank(zs, 0, width)
    blank(zs, pixels + width, width)
    fill(zs, width, slope[...].astype(f32) * adjoint[...], width)
    grads_into(acc, zs, states, width, scale, before)
    if final:
        hand_out(acc, place[1], outs, share)


def top_of(place, arrived, guess, slopes, states, before, after, image, width, scale, share):
    layers, _, pixels, channels = slopes.shape
    final = before is not None
    grad = (9, channels, channels)
    split = (2, 9, share, channels)
    tile = window((pixels, channels), (layers - 1, image), 0)
    pieces = [p for hop in arrived for p in hop]
    in_specs = [pl.BlockSpec(memory_space=pltpu.SMEM)]
    in_specs += [whole(p.shape) for p in pieces] + [whole(guess.shape), tile, tile]
    out_shape = [jax.ShapeDtypeStruct((pixels, channels), f32)]
    scratch = [pltpu.VMEM((3, pixels + 2 * width, channels), bf16)]
    if final:
        in_specs += [whole(grad), pl.BlockSpec(memory_space=pltpu.HBM)]
        out_shape += [jax.ShapeDtypeStruct(split, f32)] * (channels // share // 2)
        scratch.insert(0, pltpu.VMEM(grad, f32))
    else:
        out_shape.append(jax.ShapeDtypeStruct(grad, f32))
    return pl.pallas_call(
        functools.partial(top_kernel, width, [len(hop) for hop in arrived], final, scale, share),
        out_shape=out_shape,
        grid=(1,),
        in_specs=in_specs,
        out_specs=[whole(s.shape) for s in out_shape],
        scratch_shapes=scratch,
        cost_estimate=cost(pixels, channels, 9, pixels * channels * 20),
        compiler_params=limits(24),
        name="top",
    )(place, *pieces, guess, slopes, states, *((before, in_hbm(after)) if final else ()))


def inner_kernel(width, final, scale, share, *refs):
    place, adjoint, slope_above, slope, states, kernel = refs[:6]
    refs = list(refs[6:])
    before = refs.pop(0) if final else None
    if final:
        below, *outs, acc, zs, zs2 = refs
    else:
        below, acc, zs, zs2 = refs
    pixels = adjoint.shape[0]
    for z in (zs, zs2):
        blank(z, 0, width)
        blank(z, pixels + width, width)
    fill(zs, width, slope_above[...].astype(f32) * adjoint[...], width)
    conv_into(
        below, zs, kernel, width,
        lambda s, n, moved: adjoint[pl.ds(s, n), :] + step_size * moved,
    )
    fill(zs2, width, slope[...].astype(f32) * below[...], width)
    grads_into(acc, zs2, states, width, scale, before)
    if final:
        hand_out(acc, place[1], outs, share)


def inner_of(place, adjoint, slopes, states, kernels, before, layer, image, width, scale, share):
    pixels, channels = adjoint.shape
    final = before is not None
    grad = (9, channels, channels)
    split = (2, 9, share, channels)
    in_specs = [
        pl.BlockSpec(memory_space=pltpu.SMEM),
        whole((pixels, channels)),
        window((pixels, channels), (layer + 1, image), 0),
        window((pixels, channels), (layer, image), 0),
        window((pixels, channels), (layer, image), 0),
        pl.BlockSpec((None, *kernels.shape[1:]), lambda *_: (layer + 1, 0, 0, 0)),
    ]
    out_shape = [jax.ShapeDtypeStruct((pixels, channels), f32)]
    scratch = [pltpu.VMEM((3, pixels + 2 * width, channels), bf16)] * 2
    if final:
        in_specs.append(whole(grad))
        out_shape += [jax.ShapeDtypeStruct(split, f32)] * (channels // share // 2)
        scratch.insert(0, pltpu.VMEM(grad, f32))
    else:
        out_shape.append(jax.ShapeDtypeStruct(grad, f32))
    return pl.pallas_call(
        functools.partial(inner_kernel, width, final, scale, share),
        out_shape=out_shape,
        grid=(1,),
        in_specs=in_specs,
        out_specs=[whole(s.shape) for s in out_shape],
        scratch_shapes=scratch,
        cost_estimate=cost(pixels, channels, 18, pixels * channels * 20),
        compiler_params=limits(24),
        name="inner",
    )(place, adjoint, slopes, slopes, states, kernels, *((before,) if final else ()))


def lower_kernel(width, adjoint, slope, kernel, *refs):
    out, zs = refs[-2:]
    pixels = adjoint.shape[0]
    blank(zs, 0, width)
    blank(zs, pixels + width, width)
    fill(zs, width, slope[...].astype(f32) * adjoint[...], width)
    conv_into(
        out, zs, kernel, width,
        lambda s, n, moved: adjoint[pl.ds(s, n), :] + step_size * moved,
    )


def lower_of(adjoint, slope, kernel, image, images, into, width):
    pixels, channels = adjoint.shape
    return pl.pallas_call(
        functools.partial(lower_kernel, width),
        out_shape=jax.ShapeDtypeStruct((images, pixels, channels), f32),
        grid=(1,),
        in_specs=[
            whole((pixels, channels)),
            whole((pixels, channels)),
            whole(kernel.shape),
        ]
        + [pl.BlockSpec(memory_space=pl.ANY)] * len(into),
        out_specs=pl.BlockSpec((None, pixels, channels), lambda *_: (image, 0, 0)),
        scratch_shapes=[pltpu.VMEM((3, pixels + 2 * width, channels), bf16)],
        input_output_aliases={3: 0} if into else {},
        cost_estimate=cost(pixels, channels, 9, pixels * channels * 12),
        compiler_params=limits(16),
        name="lower",
    )(adjoint, slope, kernel, *into)


def cuts_of(height, hops):
    ends = [height * k // PIECES - 1 for k in range(1, PIECES)]
    return [[0] + [min(height, e + hops - 1 - hop) for e in ends] + [height] for hop in range(hops)]


def chain(place, ends, cuts, guess, slope, kernel, factor, width):
    sections = lax.axis_size("layer")
    images = len(ends)
    height = guess[0].shape[0] // width
    hops = sections - 1
    payload = ends
    arrivals = [[] for _ in range(images)]
    for hop in range(hops):
        pairs = [(sections - 1 - hop, sections - 2 - hop)]
        following = []
        for i in range(images):
            sent, got, tail = [], [], None
            for k, rows in enumerate(payload[i]):
                arrived = lax.ppermute(rows, "layer", pairs)
                got.append(arrived)
                if hop + 1 < hops:
                    low, high = cuts[hop][k : k + 2]
                    first, last = cuts[hop + 1][k : k + 2]
                    passed, tail = stage(
                        place, sections - 2 - hop, arrived, tail, guess[i], slope[i], kernel,
                        list(zip(cuts[0], ends[i])), factor,
                        (first, low, last, high, height), width,
                    )
                    sent.append(passed)
            following.append(sent)
            arrivals[i].append(got)
        payload = following
    return arrivals


def both_sides(pairs):
    return [(2 * a + side, 2 * b + side) for a, b in pairs for side in range(2)]


def join_kernel(items, nodes, place, mine, got, held, *outs):
    held[...] = mine[...] + got[...]
    for item, out in zip(items, outs):
        out[...] = held[which_of(item, nodes, place[2] == 0)]


def which_of(item, nodes, upward):
    high = jnp.where(upward, 1, 0)
    return high if 2 * item < nodes else 1 - high


def join(place, mine, got, items, nodes):
    block = mine.shape[1:]
    shapes = [mine.shape] + [block] * len(items)
    return pl.pallas_call(
        functools.partial(join_kernel, items, nodes),
        out_shape=[jax.ShapeDtypeStruct(x, f32) for x in shapes],
        grid=(1,),
        in_specs=[pl.BlockSpec(memory_space=pltpu.SMEM)] + [whole(mine.shape)] * 2,
        out_specs=[whole(x) for x in shapes],
        cost_estimate=pl.CostEstimate(
            flops=mine.size, bytes_accessed=16 * mine.size, transcendentals=0
        ),
        compiler_params=limits(16),
        name="join",
    )(place, mine, got)


def relay_kernel(place, held, arrived, out):
    out[...] = held[...] + arrived[...]


def relay(place, held, arrived, wave, item, nodes):
    block = arrived.shape

    def which(_, place):
        return (which_of(item, nodes, place[2] == wave - 1), 0, 0, 0)

    return pl.pallas_call(
        relay_kernel,
        out_shape=jax.ShapeDtypeStruct(block, f32),
        grid_spec=pltpu.PrefetchScalarGridSpec(
            num_scalar_prefetch=1,
            grid=(1,),
            in_specs=[pl.BlockSpec((None, *block), which), whole(block)],
            out_specs=whole(block),
        ),
        cost_estimate=pl.CostEstimate(
            flops=arrived.size, bytes_accessed=12 * arrived.size, transcendentals=0
        ),
        compiler_params=limits(12),
        name="relay",
    )(place, held, arrived)


def total_kernel(nodes, place, *refs):
    held, arrived, out = refs[: nodes // 2], refs[nodes // 2 : nodes // 2 + nodes - 1], refs[-1]
    node = place[2]
    for group, block in enumerate(held):

        @pl.when((node == group) | (node == nodes - 1 - group))
        def _(block=block):
            out[...] = block[...]

    for wave, piece in enumerate(arrived, 1):

        @pl.when((node == wave) | (node == nodes - 1 - wave))
        def _(piece=piece):
            out[...] = out[...] + piece[...]


def total(place, held, arrived, layer, layers, into):
    nodes = 2 * len(held)
    block = held[0].shape[1:]

    def which(_, place):
        return (jnp.where(2 * place[2] < nodes, 0, 1), 0, 0, 0)

    return pl.pallas_call(
        functools.partial(total_kernel, nodes),
        out_shape=jax.ShapeDtypeStruct((layers, *block), f32),
        grid_spec=pltpu.PrefetchScalarGridSpec(
            num_scalar_prefetch=1,
            grid=(1,),
            in_specs=[pl.BlockSpec((None, *block), which)] * len(held)
            + [whole(block)] * len(arrived)
            + [pl.BlockSpec(memory_space=pl.ANY)] * len(into),
            out_specs=pl.BlockSpec((None, *block), lambda *_: (layer, 0, 0, 0)),
        ),
        input_output_aliases={1 + len(held) + len(arrived): 0} if into else {},
        cost_estimate=pl.CostEstimate(
            flops=nodes * arrived[0].size, bytes_accessed=12 * arrived[0].size, transcendentals=0
        ),
        compiler_params=limits(12),
        name="total",
    )(place, *held, *arrived, *into)


def line_sum(place, terms, layer, layers, into):
    replicas = lax.axis_size("dp")
    nodes = replicas // 2
    got = []
    for group in range(nodes // 2):
        pairs = [(i, i ^ 1) for i in range(replicas)]
        got.append(lax.ppermute(terms[2 * group + 1], "dp", pairs))
    held, sends = [], {}
    for group in range(nodes // 2):
        items = [item for item in (group, nodes - 1 - group) if item < nodes - 1]
        both, *outs = join(place, terms[2 * group], got[group], items, nodes)
        held.append(both)
        sends.update(zip(items, outs))
    arrived = {}
    for wave in range(1, nodes):
        pairs = both_sides([(wave - 1, wave), (nodes - wave, nodes - 1 - wave)])
        for item in range(nodes - wave):
            out = sends[item]
            if wave > 1:
                group = held[min(item, nodes - 1 - item)]
                out = relay(place, group, arrived[wave - 1, item], wave, item, nodes)
            arrived[wave, item] = lax.ppermute(out, "dp", pairs)
    last = [arrived[wave, nodes - 1 - wave] for wave in range(1, nodes)]
    return total(place, held, last, layer, layers, into)


def plain_sum(terms):
    nodes = len(terms)
    taps, share, channels = terms[0].shape[1:]
    side = lax.axis_index("dp") % 2
    order = [(min(k, nodes - 1 - k), int(2 * k >= nodes)) for k in range(nodes)]
    mine = jnp.stack([terms[2 * group][place] for group, place in order])
    away = jnp.stack([terms[2 * group + 1][place] for group, place in order])
    first, second = jnp.where(side == 0, mine, away), jnp.where(side == 0, away, mine)
    terms = jnp.stack([first, second], axis=1).reshape(2 * nodes, taps, share, channels)
    return lax.psum_scatter(terms, "dp", scatter_dimension=0, tiled=False)


def on_device(states, slopes, kernels, guess):
    layers, images, height, width, channels = states.shape
    flat = (layers, images, height * width, channels)
    states, slopes, guess = (x.reshape(flat) for x in (states, slopes, guess))
    replicas = lax.axis_size("dp")
    sections = lax.axis_size("layer")
    share = channels // replicas
    device = lax.axis_index("dp")
    place = jnp.stack([lax.axis_index("layer"), device % 2, device // 2]).astype(jnp.int32)
    cuts = cuts_of(height, sections - 1)
    first = section_end_of(guess, slopes, kernels, 0, cuts[0][:2], width, False)
    *rest, last, slope, kernel = section_end_of(
        guess, slopes, kernels, 0, cuts[0][1:], width, True, [place]
    )
    ends, lasts, slopes_of = [[*first, *rest]], [last], [slope]
    for i in range(1, images):
        *rest, last, slope = section_end_of(guess, slopes, kernel, i, cuts[0], width, True)
        ends.append(rest)
        lasts.append(last)
        slopes_of.append(slope)
    arrivals = chain(place, ends, cuts, lasts, slopes_of, kernel, step_size * layers, width)
    scale = step_size / (images * replicas)
    adjoints = [None] * images
    grads = [None] * layers
    lower = ()
    for i in range(images):
        final = i == images - 1
        for layer in range(layers - 1, -1, -1):
            if layer == layers - 1:
                adjoints[i], *grads[layer] = top_of(
                    place, arrivals[i], lasts[i], slopes, states,
                    grads[layer][0] if final else None, lower[0] if final else None, i,
                    width, scale if final else 1.0, share,
                )
            else:
                adjoints[i], *grads[layer] = inner_of(
                    place, adjoints[i], slopes, states, kernels,
                    grads[layer][0] if final else None, layer, i, width,
                    scale if final else 1.0, share,
                )
        lower = (lower_of(adjoints[i], slopes_of[i], kernel, i, images, lower, width),)
    if replicas in (4, 8):
        gradients = ()
        for layer in range(layers - 1, -1, -1):
            gradients = (line_sum(place, grads[layer], layer, layers, gradients),)
        gradients = gradients[0]
    else:
        gradients = jnp.stack([plain_sum(grads[layer]) for layer in range(layers)])
    return lower[0].reshape(1, images, height, width, channels), gradients


def solution(mesh):
    return jax.shard_map(
        on_device,
        mesh=mesh,
        in_specs=(
            P("layer", "dp", None, None, None),
            P("layer", "dp", None, None, None),
            P("layer", None, None, None),
            P("layer", "dp", None, None, None),
        ),
        out_specs=(P("layer", "dp", None, None, None), P("layer", None, "dp", None)),
        check_vma=False,
    )
```
